32 devices in a mesh: band: 4 (over x, core), grid: 8 (over z, y).
Axes of the slice: x: 2, y: 2, z: 4, core: 2. Of those that a mesh axis runs over, the one named last changes fastest.
Arguments:
- coefficients: bfloat16 [128, 16, 15360], P('grid', None, 'band'), may hold values from -6 to 6
- block_rows: int32 [128], P('grid'), may hold values from 5 to 16
- touch_atoms: int32 [16, 16], P('grid'), may hold values from 0 to 127, as said below
- basis_values: bfloat16 [16, 256, 640], P('grid'), may hold values from -0.375 to 0.375
- outer_field: float32 [16, 640], P('grid'), may hold values from -6 to 6
- occupations: float32 [15360], P('band'), may hold values from 0 to 2
Outputs:
- gradient: float32 [128, 16, 15360], P('grid', None, 'band')
- density: float32 [16, 640], P('grid')
The draws below stay inside these ranges and needn't reach their ends.
Inputs may be any that keep to these rules, and one draw needn't show every extreme that they name: `touch_atoms`: each row names 16 different atoms. Among all entries of the 2 rows of one grid index, the atoms of each owner (atoms o * 16 to (o + 1) * 16 - 1) are named exactly 4 times or not at all.
All inputs are finite; a program needn't handle non-finite values.
Results may differ from the reference program's by a relative error of at most 0.0029.
Values may be sent and summed in bfloat16 or wider, within the bound.
No kernel may reach another device: no remote copies, remote signals or barrier semaphores. Data moves between devices by JAX's collectives and lax.ppermute only.
A program may use at most 128 MiB of HBM per device.

```python
import jax
import jax.numpy as jnp
from jax import lax

PAD_ROWS = 16
ATOM_DEV = 16
TILES_DEV = 2
TOUCH = 16
POINTS = 640
CAPACITY = 4
SLOTS = 256
BANDS = 15360
ATOMS = 128
TILES = 16


def device_touch(dev_key, owner_count):
    entries = TILES_DEV * TOUCH
    groups = entries // CAPACITY
    first, second, third = jax.random.split(dev_key, 3)
    owners = jax.random.permutation(first, owner_count)[:groups]
    group_keys = jax.random.split(second, groups)
    picks = jax.vmap(lambda k: jax.random.permutation(k, ATOM_DEV)[:CAPACITY])(group_keys)
    atoms = (owners[:, None] * ATOM_DEV + picks).reshape(entries)
    atoms = jax.random.permutation(third, atoms)
    return atoms.reshape(TILES_DEV, TOUCH).astype(jnp.int32)


def draw_touch_atoms(key, part):
    owner_count = TILES // TILES_DEV
    keys = jax.random.split(jax.random.fold_in(key, 11), owner_count)
    return jax.vmap(lambda k: device_touch(k, owner_count))(keys).reshape(TILES, TOUCH)


def draw_occupations(key, part):
    level = jnp.arange(BANDS, dtype=jnp.float32) / BANDS
    noise = jax.random.normal(jax.random.fold_in(key, 5), (BANDS,), jnp.float32)
    return 2.0 / (1.0 + jnp.exp(4.0 * level - 1.5 + 0.6 * jnp.clip(noise, -3.0, 3.0)))


def touch_ends(array, own_key, smallest, top_value):
    longest = array.shape.index(max(array.shape))
    spots = []
    for shift in (0, 1):
        where = [jax.random.randint(jax.random.fold_in(own_key, axis), (), 0, length) for axis, length in enumerate(array.shape)]
        where[longest] = (where[longest] + shift) % array.shape[longest]
        spots.append(tuple(where))
    return array.at[spots[0]].set(smallest).at[spots[1]].set(top_value)


def block_scale(stream_key, extent, shards, low, top_value):
    def one(position, shards_of):
        steps = jax.random.uniform(jax.random.fold_in(jax.random.fold_in(stream_key, 6), position), (shards_of,), jnp.float32, low / len(shards), top_value / len(shards))
        return jnp.repeat(jnp.exp(steps), extent[position] // shards_of).reshape((-1,) + (1,) * (len(extent) - position - 1))

    loudness = one(*shards[0])
    for cut in shards[1:]:
        loudness = loudness * one(*cut)
    return loudness


def centred(stream_key, extent, spread, most, cuts=(), held_as=jnp.bfloat16):
    values = spread * jax.random.normal(stream_key, extent, jnp.float32)
    if cuts:
        values = values * block_scale(stream_key, extent, cuts, -0.22, 0.18)
    return jnp.clip(values, -most, most).astype(held_as)


def setup_inputs(seed: int = 0) -> dict:
    key_of = jax.random.split(jax.random.key(seed), 7)
    coefficients = centred(key_of[0], (ATOMS, PAD_ROWS, BANDS), 1.0, 6.0, ((0, 8), (2, 4)))
    block_rows = touch_ends(jax.random.randint(key_of[1], (ATOMS,), 5, 17), jax.random.fold_in(key_of[1], 1), 5, 16).astype(jnp.int32)
    touch_atoms = draw_touch_atoms(jax.random.fold_in(key_of[6], 71), 0)
    basis_values = centred(key_of[3], (TILES, SLOTS, POINTS), SLOTS ** -0.5, 0.375, ((0, 8),))
    outer_field = centred(key_of[4], (TILES, POINTS), 1.0, 6.0, ((0, 8),), jnp.float32)
    occupations = draw_occupations(jax.random.fold_in(key_of[6], 71), 0)
    return dict(coefficients=coefficients, block_rows=block_rows, touch_atoms=touch_atoms, basis_values=basis_values, outer_field=outer_field, occupations=occupations)


exchange_coef = -0.9847450218426965


def reference(coefficients, block_rows, touch_atoms, basis_values, outer_field, occupations):
    live = (jnp.arange(PAD_ROWS, dtype=jnp.int32)[None, :] < block_rows[:, None]).astype(coefficients.dtype)
    masked = coefficients * live[:, :, None]

    def one_tile(carry, item):
        atoms, basis, outer = item
        blocks = masked[atoms].reshape(TOUCH * PAD_ROWS, BANDS)
        product = lax.dot_general(blocks, basis, (((0,), (0,)), ((), ())), preferred_element_type=jnp.float32)
        orbital = lax.optimization_barrier(product.astype(jnp.bfloat16)).astype(jnp.float32)
        density = jnp.sum(occupations[:, None] * orbital * orbital, axis=0) / BANDS
        potential = outer + exchange_coef * jnp.cbrt(density)
        wave = (occupations[:, None] * potential[None, :] * orbital).astype(jnp.bfloat16)
        projected = lax.dot_general(basis, wave, (((1,), (1,)), ((), ())), preferred_element_type=jnp.float32)
        rounded = lax.optimization_barrier(projected.astype(jnp.bfloat16))
        carry = carry.at[atoms].add(rounded.astype(jnp.float32).reshape(TOUCH, PAD_ROWS, BANDS))
        return carry, density

    start = jnp.zeros((ATOMS, PAD_ROWS, BANDS), jnp.float32)
    total, density = lax.scan(one_tile, start, (touch_atoms, basis_values, outer_field))
    return total * live[:, :, None].astype(jnp.float32), density
```

```python
import functools

import jax
import jax.numpy as jnp
from jax import lax
from jax.experimental import pallas as pl
from jax.experimental.pallas import tpu as pltpu
from jax.sharding import PartitionSpec as P

exchange_coef = -0.9847450218426965
lanes = 128
big_vmem = 60 * 1024 * 1024


def pack_kernel(groups, per, rows_ref, me_ref, coef_ref, *out_refs):
    me = me_ref[0]
    atoms, pad, _ = coef_ref.shape
    row = lax.broadcasted_iota(jnp.int32, (pad, lanes), 0)
    for d, out_ref in enumerate(out_refs):
        peer = me ^ d
        for q in range(per):
            k = peer * per + q
            start = pl.multiple_of(jnp.minimum(k, groups - 1) * lanes, lanes)
            for a in range(atoms):
                value = coef_ref[a, :, pl.ds(start, lanes)]
                limit = jnp.where(k < groups, rows_ref[a], 0)
                out_ref[a * pad : (a + 1) * pad, q * lanes : (q + 1) * lanes] = jnp.where(
                    row < limit, value, jnp.zeros_like(value)
                )


def unpack_kernel(groups, per, rows_ref, me_ref, *refs):
    in_refs, out_ref = refs[:-1], refs[-1]
    me = me_ref[0]
    atoms, pad, _ = out_ref.shape
    row = lax.broadcasted_iota(jnp.int32, (pad, lanes), 0)
    for d, in_ref in enumerate(in_refs):
        peer = me ^ d
        for q in range(per):
            k = peer * per + q

            @pl.when(k < groups)
            def _():
                start = pl.multiple_of(k * lanes, lanes)
                for a in range(atoms):
                    value = in_ref[a * pad : (a + 1) * pad, q * lanes : (q + 1) * lanes]
                    out_ref[a, :, pl.ds(start, lanes)] = jnp.where(
                        row < rows_ref[a], value.astype(jnp.float32), 0.0
                    )


def load_all(me, beta, tile_count, block_refs, basis_refs, blocks, basis, sems):
    copies = []
    pieces = len(basis_refs)
    atoms = blocks.shape[0] // len(block_refs)
    for d, ref in enumerate(block_refs):
        owner = me ^ d
        copies.append(
            pltpu.make_async_copy(ref, blocks.at[pl.ds(owner * atoms, atoms)], sems.at[d])
        )
    for e, ref in enumerate(basis_refs):
        copies.append(
            pltpu.make_async_copy(ref, basis.at[:, beta ^ e], sems.at[len(block_refs) + e])
        )
    for copy in copies:
        copy.start()
    for copy in copies:
        copy.wait()


def tile_blocks(touch_ref, tile, blocks):
    touch_len = touch_ref.shape[1]
    return jnp.concatenate([blocks[touch_ref[tile, s]] for s in range(touch_len)], axis=0)


def tile_basis(tile, tiles_dev, basis):
    owners, pieces, piece, points = basis.shape
    per = pieces // tiles_dev
    part = basis[tile // tiles_dev, pl.ds((tile % tiles_dev) * per, per)]
    return part.reshape(per * piece, points)


def forward_kernel(n, m, tiles_dev, scale, touch_ref, at_ref, weight_ref, *refs):
    block_refs, basis_refs = refs[:n], refs[n : n + m]
    out_ref, blocks, basis, sems = refs[n + m :]
    me, beta = at_ref[0], at_ref[1]
    tile_count = touch_ref.shape[0]
    load_all(me, beta, tile_count, block_refs, basis_refs, blocks, basis, sems)

    def step(tile, carry):
        part = tile_blocks(touch_ref, tile, blocks)
        product = lax.dot_general(
            part,
            tile_basis(tile, tiles_dev, basis),
            (((0,), (0,)), ((), ())),
            preferred_element_type=jnp.float32,
        )
        orbital = product.astype(jnp.bfloat16).astype(jnp.float32)
        out_ref[pl.ds(tile, 1), :] = scale * jnp.sum(
            weight_ref[...] * orbital * orbital, axis=0, keepdims=True
        )
        return carry

    lax.fori_loop(0, tile_count, step, 0)


def backward_kernel(n, m, tiles_dev, touch_ref, at_ref, weight_ref, potential_ref, *refs):
    block_refs, basis_refs = refs[:n], refs[n : n + m]
    out_refs = refs[n + m : 2 * n + m]
    blocks, basis, total, sems = refs[2 * n + m :]
    me, beta = at_ref[0], at_ref[1]
    tile_count, touch_len = touch_ref.shape
    pad = blocks.shape[1]
    load_all(me, beta, tile_count, block_refs, basis_refs, blocks, basis, sems)
    total[...] = jnp.zeros_like(total)

    def step(tile, carry):
        part = tile_blocks(touch_ref, tile, blocks)
        values = tile_basis(tile, tiles_dev, basis)
        scaled = (values.astype(jnp.float32) * potential_ref[pl.ds(tile, 1), :]).astype(
            jnp.bfloat16
        )
        couple = lax.dot_general(
            scaled, values, (((1,), (1,)), ((), ())), preferred_element_type=jnp.float32
        )
        high = couple.astype(jnp.bfloat16)
        low = (couple - high.astype(jnp.float32)).astype(jnp.bfloat16)
        piece = jnp.dot(high, part, preferred_element_type=jnp.float32) + jnp.dot(
            low, part, preferred_element_type=jnp.float32
        )
        for s in range(touch_len):
            total[touch_ref[tile, s]] += piece[s * pad : (s + 1) * pad]
        return carry

    lax.fori_loop(0, tile_count, step, 0)
    weight = weight_ref[...]
    atoms = blocks.shape[0] // n
    for d, out_ref in enumerate(out_refs):
        owner = me ^ d
        for a in range(atoms):
            out_ref[a * pad : (a + 1) * pad, :] = (total[owner * atoms + a] * weight).astype(
                jnp.bfloat16
            )


smem = pl.BlockSpec(memory_space=pltpu.SMEM)
vmem = pl.BlockSpec(memory_space=pltpu.VMEM)
anywhere = pl.BlockSpec(memory_space=pl.ANY)


def swap(value, axis, offset):
    size = lax.axis_size(axis)
    return lax.ppermute(value, axis, [(i, i ^ offset) for i in range(size)])


def exchange(parts):
    return [parts[0]] + [swap(parts[d], "grid", d) for d in range(1, len(parts))]


def all_sum(value):
    for axis in ("band", "grid"):
        offset = 1
        while offset < lax.axis_size(axis):
            value = value + swap(value, axis, offset)
            offset *= 2
    return value


def body(coefficients, block_rows, touch_atoms, basis_values, outer_field, occupations):
    n = lax.axis_size("grid")
    m = lax.axis_size("band")
    me = lax.axis_index("grid").astype(jnp.int32)
    beta = lax.axis_index("band").astype(jnp.int32)
    atoms, pad, band_dev = coefficients.shape
    tiles_dev, touch_len = touch_atoms.shape
    points = basis_values.shape[2]
    slots = basis_values.shape[1]
    tile_count = tiles_dev * n
    groups = band_dev // lanes
    per = (groups + n - 1) // n
    width = per * lanes
    params = pltpu.CompilerParams(vmem_limit_bytes=big_vmem)
    at = jnp.stack([me, beta])

    touch_all = lax.all_gather(touch_atoms, "grid", axis=0, tiled=True)
    outer_all = lax.all_gather(outer_field, "grid", axis=0, tiled=True)

    piece = tiles_dev * slots // m
    own = lax.dynamic_slice_in_dim(
        basis_values.reshape(tiles_dev * slots, points), beta * piece, piece, 0
    )
    spread = lax.all_to_all(
        jnp.broadcast_to(own[None], (n, piece, points)), "grid", split_axis=0, concat_axis=0, tiled=True
    )

    sent = pl.pallas_call(
        functools.partial(pack_kernel, groups, per),
        out_shape=[jax.ShapeDtypeStruct((atoms * pad, width), jnp.bfloat16)] * n,
        in_specs=[smem, smem, vmem],
        out_specs=[vmem] * n,
        compiler_params=params,
        name="pack",
    )(block_rows, at, coefficients)
    got = [item.reshape(atoms, pad, width) for item in exchange(sent)]

    pieces = [spread]
    offset = m // 2
    order = [0]
    while offset:
        pieces = pieces + [swap(item, "band", offset) for item in pieces]
        order = order + [e ^ offset for e in order]
        offset //= 2
    basis = [pieces[order.index(e)] for e in range(m)]

    filled = jnp.pad(occupations, (0, n * width - band_dev))
    weight = lax.dynamic_slice_in_dim(filled, me * width, width, 0)
    all_bands = band_dev * m
    scratch = [
        pltpu.VMEM((n * atoms, pad, width), jnp.bfloat16),
        pltpu.VMEM((n, m, piece, points), jnp.bfloat16),
    ]
    sems = pltpu.SemaphoreType.DMA((n + m,))
    partial_value = pl.pallas_call(
        functools.partial(forward_kernel, n, m, tiles_dev, 1.0 / all_bands),
        out_shape=jax.ShapeDtypeStruct((tile_count, points), jnp.float32),
        in_specs=[smem, smem, vmem] + [anywhere] * (n + m),
        out_specs=vmem,
        scratch_shapes=scratch + [sems],
        compiler_params=params,
        name="forward",
    )(touch_all, at, weight[:, None], *got, *basis)
    density = all_sum(partial_value)
    potential = outer_all + exchange_coef * jnp.cbrt(density)
    back = pl.pallas_call(
        functools.partial(backward_kernel, n, m, tiles_dev),
        out_shape=[jax.ShapeDtypeStruct((atoms * pad, width), jnp.bfloat16)] * n,
        in_specs=[smem, smem, vmem, vmem] + [anywhere] * (n + m),
        out_specs=[vmem] * n,
        scratch_shapes=scratch + [pltpu.VMEM((n * atoms, pad, width), jnp.float32), sems],
        compiler_params=params,
        name="backward",
    )(touch_all, at, weight[None, :], potential, *got, *basis)
    returned = exchange(back)
    gradient = pl.pallas_call(
        functools.partial(unpack_kernel, groups, per),
        out_shape=jax.ShapeDtypeStruct((atoms, pad, band_dev), jnp.float32),
        in_specs=[smem, smem] + [vmem] * n,
        out_specs=vmem,
        compiler_params=params,
        name="unpack",
    )(block_rows, at, *returned)
    own_density = lax.dynamic_slice_in_dim(density, me * tiles_dev, tiles_dev, 0)
    return (gradient, own_density)


def solution(mesh):
    placed = (
        P("grid", None, "band"),
        P("grid"),
        P("grid", None),
        P("grid", None, None),
        P("grid", None),
        P("band"),
    )
    return jax.shard_map(
        body,
        mesh=mesh,
        in_specs=placed,
        out_specs=(P("grid", None, "band"), P("grid", None)),
        check_vma=False,
    )
```

```python
import functools

import jax
import jax.numpy as jnp
from jax import lax
from jax.experimental import pallas as pl
from jax.experimental.pallas import tpu as pltpu
from jax.sharding import PartitionSpec as P

exchange_coef = -0.9847450218426965
lanes = 128
big_vmem = 60 * 1024 * 1024


def pack_kernel(groups, per, rows_ref, me_ref, coef_ref, *out_refs):
    me = me_ref[0]
    atoms, pad, _ = coef_ref.shape
    row = lax.broadcasted_iota(jnp.int32, (pad, lanes), 0)
    for d, out_ref in enumerate(out_refs):
        peer = me ^ d
        for q in range(per):
            k = peer * per + q
            start = pl.multiple_of(jnp.minimum(k, groups - 1) * lanes, lanes)
            for a in range(atoms):
                value = coef_ref[a, :, pl.ds(start, lanes)]
                limit = jnp.where(k < groups, rows_ref[a], 0)
                out_ref[a * pad : (a + 1) * pad, q * lanes : (q + 1) * lanes] = jnp.where(
                    row < limit, value, jnp.zeros_like(value)
                )


def unpack_kernel(groups, per, rows_ref, me_ref, *refs):
    in_refs, out_ref = refs[:-1], refs[-1]
    me = me_ref[0]
    atoms, pad, _ = out_ref.shape
    row = lax.broadcasted_iota(jnp.int32, (pad, lanes), 0)
    for d, in_ref in enumerate(in_refs):
        peer = me ^ d
        for q in range(per):
            k = peer * per + q

            @pl.when(k < groups)
            def _():
                start = pl.multiple_of(k * lanes, lanes)
                for a in range(atoms):
                    value = in_ref[a * pad : (a + 1) * pad, q * lanes : (q + 1) * lanes]
                    out_ref[a, :, pl.ds(start, lanes)] = jnp.where(
                        row < rows_ref[a], value.astype(jnp.float32), 0.0
                    )


def prep_kernel(piece, at_ref, touch_ref, rows_ref, outer_ref, basis_ref, out_ref, meta):
    beta = at_ref[1]
    tiles_dev, touch_len = touch_ref.shape
    atoms = rows_ref.shape[1]
    start = pl.multiple_of(beta * piece, piece)
    out_ref[:piece] = basis_ref[pl.ds(start, piece), :]
    meta[...] = jnp.zeros_like(meta)
    rest = outer_ref[...]
    for part in range(3):
        rounded = rest.astype(jnp.bfloat16).astype(jnp.float32)
        meta[part * tiles_dev : (part + 1) * tiles_dev, :] = rounded
        rest = rest - rounded
    ids = touch_ref[...]
    row = 3 * tiles_dev
    meta[row : row + tiles_dev, :touch_len] = (ids & 255).astype(jnp.float32)
    row += tiles_dev
    meta[row : row + tiles_dev, :touch_len] = (ids >> 8).astype(jnp.float32)
    row += tiles_dev
    meta[row : row + 1, :atoms] = rows_ref[...].astype(jnp.float32)
    out_ref[piece:] = meta[...].astype(jnp.bfloat16)


def load_all(block_refs, basis_refs, blocks, basis, sems):
    n, (low, m) = len(block_refs), basis.shape[:2]
    atoms = blocks.shape[0] // n
    copies = []
    for d, ref in enumerate(block_refs):
        copies.append(
            pltpu.make_async_copy(ref, blocks.at[pl.ds(d * atoms, atoms)], sems.at[d])
        )
    for y in range(low):
        for e in range(m):
            k = y * m + e
            copies.append(pltpu.make_async_copy(basis_refs[k], basis.at[y, e], sems.at[n + k]))
    for copy in copies:
        copy.start()
    for copy in copies:
        copy.wait()


def tile_blocks(touch_ref, me, index, blocks, atoms):
    touch_len = touch_ref.shape[1]
    return jnp.concatenate(
        [blocks[touch_ref[index, s] ^ (me * atoms)] for s in range(touch_len)], axis=0
    )


def tile_basis(beta, index, tiles_dev, piece, basis):
    low, m = basis.shape[:2]
    d, slot = index // tiles_dev, index % tiles_dev
    count = m // tiles_dev
    return jnp.concatenate(
        [basis[d % low, (slot * count + c) ^ beta, d // low, :piece] for c in range(count)], axis=0
    )


def global_tile(me, index, tiles_dev):
    return ((index // tiles_dev) ^ me) * tiles_dev + index % tiles_dev


def forward_kernel(n, k, tiles_dev, piece, scale, touch_ref, at_ref, weight_ref, *refs):
    block_refs, basis_refs = refs[:n], refs[n : n + k]
    out_ref, blocks, basis, sems = refs[n + k :]
    me, beta = at_ref[0], at_ref[1]
    tile_count = touch_ref.shape[0]
    atoms = blocks.shape[0] // n
    load_all(block_refs, basis_refs, blocks, basis, sems)

    def step(index, carry):
        part = tile_blocks(touch_ref, me, index, blocks, atoms)
        product = lax.dot_general(
            part,
            tile_basis(beta, index, tiles_dev, piece, basis),
            (((0,), (0,)), ((), ())),
            preferred_element_type=jnp.float32,
        )
        orbital = product.astype(jnp.bfloat16).astype(jnp.float32)
        out_ref[pl.ds(global_tile(me, index, tiles_dev), 1), :] = scale * jnp.sum(
            weight_ref[...] * orbital * orbital, axis=0, keepdims=True
        )
        return carry

    lax.fori_loop(0, tile_count, step, 0)


def backward_kernel(n, k, tiles_dev, piece, touch_ref, at_ref, weight_ref, outer_ref, local_ref, *refs):
    block_refs, basis_refs = refs[:n], refs[n : n + k]
    out_refs = refs[n + k : 2 * n + k]
    blocks, basis, total, sems = refs[2 * n + k :]
    me, beta = at_ref[0], at_ref[1]
    tile_count, touch_len = touch_ref.shape
    pad = blocks.shape[1]
    atoms = blocks.shape[0] // n
    load_all(block_refs, basis_refs, blocks, basis, sems)
    total[...] = jnp.zeros_like(total)

    def step(index, carry):
        part = tile_blocks(touch_ref, me, index, blocks, atoms)
        values = tile_basis(beta, index, tiles_dev, piece, basis)
        potential = (
            outer_ref[pl.ds(index, 1), :]
            + local_ref[pl.ds(global_tile(me, index, tiles_dev), 1), :]
        )
        scaled = (values.astype(jnp.float32) * potential).astype(jnp.bfloat16)
        couple = lax.dot_general(
            scaled, values, (((1,), (1,)), ((), ())), preferred_element_type=jnp.float32
        )
        high = couple.astype(jnp.bfloat16)
        low = (couple - high.astype(jnp.float32)).astype(jnp.bfloat16)
        product = jnp.dot(high, part, preferred_element_type=jnp.float32) + jnp.dot(
            low, part, preferred_element_type=jnp.float32
        )
        for s in range(touch_len):
            total[touch_ref[index, s] ^ (me * atoms)] += product[s * pad : (s + 1) * pad]
        return carry

    lax.fori_loop(0, tile_count, step, 0)
    weight = weight_ref[...]
    for d, out_ref in enumerate(out_refs):
        for a in range(atoms):
            out_ref[a * pad : (a + 1) * pad, :] = (total[d * atoms + a] * weight).astype(
                jnp.bfloat16
            )


smem = pl.BlockSpec(memory_space=pltpu.SMEM)
vmem = pl.BlockSpec(memory_space=pltpu.VMEM)
anywhere = pl.BlockSpec(memory_space=pl.ANY)


def swap(value, axis, offset):
    size = lax.axis_size(axis)
    return lax.ppermute(value, axis, [(i, i ^ offset) for i in range(size)])


def exchange(parts):
    return [parts[0]] + [swap(parts[d], "grid", d) for d in range(1, len(parts))]


def all_sum(value):
    for axis in ("band", "grid"):
        offset = 1
        while offset < lax.axis_size(axis):
            value = value + swap(value, axis, offset)
            offset *= 2
    return value


def body(coefficients, block_rows, touch_atoms, basis_values, outer_field, occupations):
    n = lax.axis_size("grid")
    m = lax.axis_size("band")
    me = lax.axis_index("grid").astype(jnp.int32)
    beta = lax.axis_index("band").astype(jnp.int32)
    atoms, pad, band_dev = coefficients.shape
    tiles_dev, touch_len = touch_atoms.shape
    points = basis_values.shape[2]
    slots = basis_values.shape[1]
    tile_count = tiles_dev * n
    groups = band_dev // lanes
    per = (groups + n - 1) // n
    width = per * lanes
    params = pltpu.CompilerParams(vmem_limit_bytes=big_vmem)
    at = jnp.stack([me, beta])

    piece = tiles_dev * slots // m
    extra = -(-(5 * tiles_dev + 1) // 16) * 16
    low = 1 << ((n.bit_length() - 1) // 2)
    message = pl.pallas_call(
        functools.partial(prep_kernel, piece),
        out_shape=jax.ShapeDtypeStruct((piece + extra, points), jnp.bfloat16),
        in_specs=[smem, vmem, vmem, vmem, vmem],
        out_specs=vmem,
        scratch_shapes=[pltpu.VMEM((extra, points), jnp.float32)],
        compiler_params=params,
        name="prep",
    )(
        at,
        touch_atoms,
        block_rows.reshape(1, atoms),
        outer_field,
        basis_values.reshape(tiles_dev * slots, points),
    )
    column = [message] + [swap(message, "grid", low * k) for k in range(1, n // low)]

    sent = pl.pallas_call(
        functools.partial(pack_kernel, groups, per),
        out_shape=[jax.ShapeDtypeStruct((atoms * pad, width), jnp.bfloat16)] * n,
        in_specs=[smem, smem, vmem],
        out_specs=[vmem] * n,
        compiler_params=params,
        name="pack",
    )(block_rows, at, coefficients)
    column, sent = lax.optimization_barrier((jnp.stack(column), sent))
    pieces = {(0, 0): column}
    for x in range(2, m, 2):
        pieces[0, x] = swap(column, "band", x)
    for y in range(1, low):
        pieces[y, 0] = swap(column, "grid", y)
    got = [item.reshape(atoms, pad, width) for item in exchange(sent)]
    for y in range(1, low):
        for x in range(2, m, 2):
            pieces[y, x] = swap(pieces[0, x], "grid", y)
    for y, x in list(pieces):
        pieces[y, x + 1] = swap(pieces[y, x], "band", 1)
    basis = [pieces[y, e] for y in range(low) for e in range(m)]
    tables = jnp.stack([pieces[d % low, 0][d // low, piece:] for d in range(n)]).astype(jnp.float32)
    part = tables[:, : 3 * tiles_dev].reshape(n, 3, tiles_dev, points)
    outer = (part[:, 0] + part[:, 1] + part[:, 2]).reshape(tile_count, points)
    ids = tables[:, 3 * tiles_dev : 5 * tiles_dev, :touch_len].reshape(n, 2, tiles_dev, touch_len)
    touch = (ids[:, 0] + 256.0 * ids[:, 1]).astype(jnp.int32).reshape(tile_count, touch_len)

    filled = jnp.pad(occupations, (0, n * width - band_dev))
    weight = lax.dynamic_slice_in_dim(filled, me * width, width, 0)
    all_bands = band_dev * m
    scratch = [
        pltpu.VMEM((n * atoms, pad, width), jnp.bfloat16),
        pltpu.VMEM((low, m, n // low, piece + extra, points), jnp.bfloat16),
    ]
    count = low * m
    sems = pltpu.SemaphoreType.DMA((n + count,))
    partial_value = pl.pallas_call(
        functools.partial(forward_kernel, n, count, tiles_dev, piece, 1.0 / all_bands),
        out_shape=jax.ShapeDtypeStruct((tile_count, points), jnp.float32),
        in_specs=[smem, smem, vmem] + [anywhere] * (n + count),
        out_specs=vmem,
        scratch_shapes=scratch + [sems],
        compiler_params=params,
        name="forward",
    )(touch, at, weight[:, None], *got, *basis)
    density = all_sum(partial_value)
    local = exchange_coef * jnp.cbrt(density)
    back = pl.pallas_call(
        functools.partial(backward_kernel, n, count, tiles_dev, piece),
        out_shape=[jax.ShapeDtypeStruct((atoms * pad, width), jnp.bfloat16)] * n,
        in_specs=[smem, smem, vmem, vmem, vmem] + [anywhere] * (n + count),
        out_specs=[vmem] * n,
        scratch_shapes=scratch + [pltpu.VMEM((n * atoms, pad, width), jnp.float32), sems],
        compiler_params=params,
        name="backward",
    )(touch, at, weight[None, :], outer, local, *got, *basis)
    returned = exchange(back)
    gradient = pl.pallas_call(
        functools.partial(unpack_kernel, groups, per),
        out_shape=jax.ShapeDtypeStruct((atoms, pad, band_dev), jnp.float32),
        in_specs=[smem, smem] + [vmem] * n,
        out_specs=vmem,
        compiler_params=params,
        name="unpack",
    )(block_rows, at, *returned)
    own_density = lax.dynamic_slice_in_dim(density, me * tiles_dev, tiles_dev, 0)
    return (gradient, own_density)


def solution(mesh):
    placed = (
        P("grid", None, "band"),
        P("grid"),
        P("grid", None),
        P("grid", None, None),
        P("grid", None),
        P("band"),
    )
    return jax.shard_map(
        body,
        mesh=mesh,
        in_specs=placed,
        out_specs=(P("grid", None, "band"), P("grid", None)),
        check_vma=False,
    )
```

```python
import functools

import jax
import jax.numpy as jnp
from jax import lax
from jax.experimental import pallas as pl
from jax.experimental.pallas import tpu as pltpu
from jax.sharding import PartitionSpec as P

exchange_coef = -0.9847450218426965
lanes = 128
big_vmem = 60 * 1024 * 1024


def gather_matrix(rows, atoms, pad):
    count = atoms * pad
    lane = lax.broadcasted_iota(jnp.int32, (1, count), 1)
    place = jnp.full((1, count), -1, jnp.int32)
    start = 0
    for a in range(atoms):
        inner = lane - a * pad
        place = jnp.where((inner >= 0) & (inner < rows(a)), start + inner, place)
        start = start + rows(a)
    packed = lax.broadcasted_iota(jnp.int32, (count, count), 0)
    return jnp.where(packed == place, 1.0, 0.0).astype(jnp.bfloat16)


def spread_matrix(rows, atoms, pad):
    inner = lax.broadcasted_iota(jnp.int32, (pad, atoms * pad), 0)
    packed = lax.broadcasted_iota(jnp.int32, (pad, atoms * pad), 1)
    parts = []
    start = 0
    for a in range(atoms):
        parts.append(jnp.where((packed == start + inner) & (inner < rows(a)), 1.0, 0.0))
        start = start + rows(a)
    return jnp.concatenate(parts, axis=0).astype(jnp.bfloat16)


def pack_kernel(groups, per, rows_ref, coef_ref, main_ref, spill_ref):
    atoms, pad, band_dev = coef_ref.shape
    n, keep, width = main_ref.shape
    matrix = gather_matrix(lambda a: rows_ref[a], atoms, pad)
    for j in range(n):
        used = max(0, min(width, band_dev - j * width))
        if used:
            value = coef_ref[:, :, j * width : j * width + used].reshape(atoms * pad, used)
            packed = jnp.dot(matrix, value, preferred_element_type=jnp.float32)
            packed = packed.astype(jnp.bfloat16)
            main_ref[j, :, :used] = packed[:keep]
            spill_ref[j, :, :used] = packed[keep:]
        if used < width:
            main_ref[j, :, used:] = jnp.zeros((keep, width - used), jnp.bfloat16)
            spill_ref[j, :, used:] = jnp.zeros((atoms * pad - keep, width - used), jnp.bfloat16)


def unpack_kernel(groups, per, rows_ref, at_ref, spill_ref, *refs):
    in_refs, out_ref = refs[:-1], refs[-1]
    me = at_ref[0]
    atoms, pad, _ = out_ref.shape
    matrix = spread_matrix(lambda a: rows_ref[a], atoms, pad)
    for d, in_ref in enumerate(in_refs):
        peer = me ^ d
        packed = jnp.concatenate([in_ref[...], spill_ref[peer]], axis=0)
        value = jnp.dot(matrix, packed, preferred_element_type=jnp.float32)
        for q in range(per):
            k = peer * per + q

            @pl.when(k < groups)
            def _():
                start = pl.multiple_of(k * lanes, lanes)
                piece = value[:, q * lanes : (q + 1) * lanes]
                out_ref[:, :, pl.ds(start, lanes)] = piece.reshape(atoms, pad, lanes)


def prep_kernel(piece, at_ref, touch_ref, rows_ref, outer_ref, basis_ref, out_ref, meta):
    beta = at_ref[1]
    tiles_dev, touch_len = touch_ref.shape
    atoms = rows_ref.shape[1]
    start = pl.multiple_of(beta * piece, piece)
    out_ref[:piece] = basis_ref[pl.ds(start, piece), :]
    meta[...] = jnp.zeros_like(meta)
    rest = outer_ref[...]
    for part in range(3):
        rounded = rest.astype(jnp.bfloat16).astype(jnp.float32)
        meta[part * tiles_dev : (part + 1) * tiles_dev, :] = rounded
        rest = rest - rounded
    ids = touch_ref[...]
    row = 3 * tiles_dev
    meta[row : row + tiles_dev, :touch_len] = (ids & 255).astype(jnp.float32)
    row += tiles_dev
    meta[row : row + tiles_dev, :touch_len] = (ids >> 8).astype(jnp.float32)
    row += tiles_dev
    meta[row : row + 1, :atoms] = rows_ref[...].astype(jnp.float32)
    out_ref[piece:] = meta[...].astype(jnp.bfloat16)


def load_basis(basis_refs, basis, sems):
    _, m, size = basis.shape[:3]
    copies = []
    chunk = basis_refs[0].shape[0]
    halves = size // chunk
    for index, ref in enumerate(basis_refs):
        half, y, e = index % halves, index // halves // m, index // halves % m
        target = basis.at[y, e, half * chunk : (half + 1) * chunk]
        copies.append(pltpu.make_async_copy(ref, target, sems.at[index]))
    for copy in copies:
        copy.start()
    return copies


def tile_blocks(touch_ref, index, blocks):
    atoms, touch_len = blocks.shape[1], touch_ref.shape[1]
    ids = [touch_ref[index, s] for s in range(touch_len)]
    return jnp.concatenate([blocks[a // atoms, a % atoms] for a in ids], axis=0)


def tile_basis(beta, index, tiles_dev, piece, basis):
    low, m = basis.shape[:2]
    d, slot = index // tiles_dev, index % tiles_dev
    count = m // tiles_dev
    return jnp.concatenate(
        [basis[d % low, (slot * count + c) ^ beta, d // low, :piece] for c in range(count)], axis=0
    )


def global_tile(me, index, tiles_dev):
    return ((index // tiles_dev) ^ me) * tiles_dev + index % tiles_dev


def forward_kernel(
    n, k, tiles_dev, piece, scale, touch_ref, rows_ref, at_ref, weight_ref, main_ref, spill_ref, *refs
):
    basis_refs, (out_ref, blocks, basis, sems) = refs[:k], refs[k:]
    me, beta = at_ref[0], at_ref[1]
    tile_count = touch_ref.shape[0]
    _, atoms, pad, width = blocks.shape
    copies = load_basis(basis_refs, basis, sems)
    for d in range(n):
        owner = me ^ d
        matrix = spread_matrix(lambda a: rows_ref[d, a], atoms, pad)
        packed = jnp.concatenate([main_ref[owner], spill_ref[owner]], axis=0)
        value = jnp.dot(matrix, packed, preferred_element_type=jnp.float32)
        blocks[owner] = value.astype(jnp.bfloat16).reshape(atoms, pad, width)
    for copy in copies:
        copy.wait()

    def step(index, carry):
        part = tile_blocks(touch_ref, index, blocks)
        product = lax.dot_general(
            part,
            tile_basis(beta, index, tiles_dev, piece, basis),
            (((0,), (0,)), ((), ())),
            preferred_element_type=jnp.float32,
        )
        orbital = product.astype(jnp.bfloat16).astype(jnp.float32)
        out_ref[pl.ds(global_tile(me, index, tiles_dev), 1), :] = scale * jnp.sum(
            weight_ref[...] * orbital * orbital, axis=0, keepdims=True
        )
        return carry

    lax.fori_loop(0, tile_count, step, 0, unroll=4)


def backward_kernel(
    n, k, tiles_dev, piece, touch_ref, rows_ref, at_ref, weight_ref, outer_ref, local_ref, *refs
):
    basis_refs, block_ref = refs[:k], refs[k]
    out_refs = refs[k + 1 : k + 1 + n]
    spill_ref, blocks, basis, total, sems = refs[k + 1 + n :]
    me, beta = at_ref[0], at_ref[1]
    tile_count, touch_len = touch_ref.shape
    _, atoms, pad, width = blocks.shape
    copies = load_basis(basis_refs, basis, sems)
    copies.append(pltpu.make_async_copy(block_ref, blocks, sems.at[k]))
    copies[-1].start()
    total[...] = jnp.zeros_like(total)
    weight = weight_ref[...]
    for copy in copies:
        copy.wait()

    def step(index, carry):
        part = tile_blocks(touch_ref, index, blocks)
        values = tile_basis(beta, index, tiles_dev, piece, basis)
        potential = (
            outer_ref[pl.ds(index, 1), :]
            + local_ref[pl.ds(global_tile(me, index, tiles_dev), 1), :]
        )
        scaled = (values.astype(jnp.float32) * potential).astype(jnp.bfloat16)
        couple = lax.dot_general(
            scaled, values, (((1,), (1,)), ((), ())), preferred_element_type=jnp.float32
        )
        high = couple.astype(jnp.bfloat16)
        low = (couple - high.astype(jnp.float32)).astype(jnp.bfloat16)
        product = jnp.dot(high, part, preferred_element_type=jnp.float32) + jnp.dot(
            low, part, preferred_element_type=jnp.float32
        )
        product = (weight * product).astype(jnp.bfloat16).astype(jnp.float32)
        for s in range(touch_len):
            total[touch_ref[index, s]] += product[s * pad : (s + 1) * pad]
        return carry

    lax.fori_loop(0, tile_count, step, 0, unroll=4)
    for d, out_ref in enumerate(out_refs):
        owner = me ^ d
        matrix = gather_matrix(lambda a: rows_ref[d, a], atoms, pad)
        value = total[pl.ds(owner * atoms, atoms)].astype(jnp.bfloat16).reshape(atoms * pad, width)
        packed = jnp.dot(matrix, value, preferred_element_type=jnp.float32).astype(jnp.bfloat16)
        out_ref[...] = packed[: out_ref.shape[0]]
        spill_ref[owner] = packed[out_ref.shape[0] :]


smem = pl.BlockSpec(memory_space=pltpu.SMEM)
vmem = pl.BlockSpec(memory_space=pltpu.VMEM)
anywhere = pl.BlockSpec(memory_space=pl.ANY)


def swap(value, axis, offset):
    size = lax.axis_size(axis)
    return lax.ppermute(value, axis, [(i, i ^ offset) for i in range(size)])


def exchange(parts):
    return [parts[0]] + [swap(parts[d], "grid", d) for d in range(1, len(parts))]


def all_sum(value):
    for axis in ("band", "grid"):
        offset = 1
        while offset < lax.axis_size(axis):
            value = value + swap(value, axis, offset)
            offset *= 2
    return value


def body(coefficients, block_rows, touch_atoms, basis_values, outer_field, occupations):
    n = lax.axis_size("grid")
    m = lax.axis_size("band")
    me = lax.axis_index("grid").astype(jnp.int32)
    beta = lax.axis_index("band").astype(jnp.int32)
    atoms, pad, band_dev = coefficients.shape
    tiles_dev, touch_len = touch_atoms.shape
    points = basis_values.shape[2]
    slots = basis_values.shape[1]
    tile_count = tiles_dev * n
    groups = band_dev // lanes
    per = (groups + n - 1) // n
    width = per * lanes
    params = pltpu.CompilerParams(vmem_limit_bytes=big_vmem)
    at = jnp.stack([me, beta])

    keep = atoms * pad * 13 // 16

    def across(value):
        return lax.all_to_all(value, "grid", split_axis=0, concat_axis=0, tiled=True)

    piece = tiles_dev * slots // m
    extra = -(-(5 * tiles_dev + 1) // 16) * 16
    low = 1 << ((n.bit_length() - 1) // 2)
    message = pl.pallas_call(
        functools.partial(prep_kernel, piece),
        out_shape=jax.ShapeDtypeStruct((piece + extra, points), jnp.bfloat16),
        in_specs=[smem, vmem, vmem, vmem, vmem],
        out_specs=vmem,
        scratch_shapes=[pltpu.VMEM((extra, points), jnp.float32)],
        compiler_params=params,
        name="prep",
    )(
        at,
        touch_atoms,
        block_rows.reshape(1, atoms),
        outer_field,
        basis_values.reshape(tiles_dev * slots, points),
    )
    size = n // low
    half = max(1, size // 2)
    pieces = {}

    def widen(h):
        for y in range(1, low):
            pieces[y, 0, h] = swap(pieces[0, 0, h], "grid", y)

    column = [message] + [swap(message, "grid", low * k) for k in range(1, size)]
    sent, spill = pl.pallas_call(
        functools.partial(pack_kernel, groups, per),
        out_shape=[
            jax.ShapeDtypeStruct((n, keep, width), jnp.bfloat16),
            jax.ShapeDtypeStruct((n, atoms * pad - keep, width), jnp.bfloat16),
        ],
        in_specs=[smem, vmem],
        out_specs=[vmem, vmem],
        compiler_params=params,
        name="pack",
    )(block_rows, coefficients)
    near, sent, spill = lax.optimization_barrier((column[:half], sent, spill))
    pieces[0, 0, 0] = jnp.stack(near)
    widen(0)
    sent, column, pieces = lax.optimization_barrier((sent, column, pieces))
    got = across(sent)
    parts = range(0, size, half)
    for h in parts[1:]:
        pieces[0, 0, h] = jnp.stack(column[h : h + half])
        widen(h)
    for h in parts:
        for y in range(low):
            for x in range(2, m, 2):
                pieces[y, x, h] = swap(pieces[y, 0, h], "band", x)
    for y, x, h in list(pieces):
        pieces[y, x + 1, h] = swap(pieces[y, x, h], "band", 1)
    basis = [pieces[y, e, h] for y in range(low) for e in range(m) for h in parts]
    tables = [pieces[d % low, 0, d // low // half * half][d // low % half, piece:] for d in range(n)]
    tables = jnp.stack(tables).astype(jnp.float32)
    part = tables[:, : 3 * tiles_dev].reshape(n, 3, tiles_dev, points)
    outer = (part[:, 0] + part[:, 1] + part[:, 2]).reshape(tile_count, points)
    ids = tables[:, 3 * tiles_dev : 5 * tiles_dev, :touch_len].reshape(n, 2, tiles_dev, touch_len)
    touch = (ids[:, 0] + 256.0 * ids[:, 1]).astype(jnp.int32).reshape(tile_count, touch_len)

    rows = tables[:, 5 * tiles_dev, :atoms].astype(jnp.int32)
    more = jnp.any(jnp.sum(rows, axis=1) > keep)
    more, spill, got = lax.optimization_barrier((more, spill, got))

    def rest(value):
        return lax.cond(more, across, lambda same: same, value)

    filled = jnp.pad(occupations, (0, n * width - band_dev))
    weight = lax.dynamic_slice_in_dim(filled, me * width, width, 0)
    all_bands = band_dev * m
    scratch = [
        pltpu.VMEM((n, atoms, pad, width), jnp.bfloat16),
        pltpu.VMEM((low, m, n // low, piece + extra, points), jnp.bfloat16),
    ]
    count = len(basis)
    sems = pltpu.SemaphoreType.DMA((1 + count,))
    partial_value, blocks = pl.pallas_call(
        functools.partial(forward_kernel, n, count, tiles_dev, piece, 1.0 / all_bands),
        out_shape=[
            jax.ShapeDtypeStruct((tile_count, points), jnp.float32),
            jax.ShapeDtypeStruct((n, atoms, pad, width), jnp.bfloat16),
        ],
        in_specs=[smem, smem, smem, vmem, vmem, vmem] + [anywhere] * count,
        out_specs=[vmem, vmem],
        scratch_shapes=scratch[1:] + [sems],
        compiler_params=params,
        name="forward",
    )(touch, rows, at, weight[:, None], got, rest(spill), *basis)
    density = all_sum(partial_value)
    local = exchange_coef * jnp.cbrt(density)
    *back, spill = pl.pallas_call(
        functools.partial(backward_kernel, n, count, tiles_dev, piece),
        out_shape=[jax.ShapeDtypeStruct((keep, width), jnp.bfloat16)] * n
        + [jax.ShapeDtypeStruct((n, atoms * pad - keep, width), jnp.bfloat16)],
        in_specs=[smem, smem, smem, vmem, vmem, vmem] + [anywhere] * (1 + count),
        out_specs=[vmem] * (n + 1),
        scratch_shapes=scratch + [pltpu.VMEM((n * atoms, pad, width), jnp.float32), sems],
        compiler_params=params,
        name="backward",
    )(touch, rows, at, weight[None, :], outer, local, *basis, blocks)
    returned = exchange(back)
    gradient = pl.pallas_call(
        functools.partial(unpack_kernel, groups, per),
        out_shape=jax.ShapeDtypeStruct((atoms, pad, band_dev), jnp.float32),
        in_specs=[smem, smem] + [vmem] * (n + 1),
        out_specs=vmem,
        compiler_params=params,
        name="unpack",
    )(block_rows, at, rest(spill), *returned)
    own_density = lax.dynamic_slice_in_dim(density, me * tiles_dev, tiles_dev, 0)
    return (gradient, own_density)


def solution(mesh):
    placed = (
        P("grid", None, "band"),
        P("grid"),
        P("grid", None),
        P("grid", None, None),
        P("grid", None),
        P("band"),
    )
    return jax.shard_map(
        body,
        mesh=mesh,
        in_specs=placed,
        out_specs=(P("grid", None, "band"), P("grid", None)),
        check_vma=False,
    )
```

```python
import functools

import jax
import jax.numpy as jnp
from jax import lax
from jax.experimental import pallas as pl
from jax.experimental.pallas import tpu as pltpu
from jax.sharding import PartitionSpec as P

exchange_coef = -0.9847450218426965
lanes = 128
big_vmem = 60 * 1024 * 1024


def gather_matrix(rows, atoms, pad):
    count = atoms * pad
    lane = lax.broadcasted_iota(jnp.int32, (1, count), 1)
    place = jnp.full((1, count), -1, jnp.int32)
    start = 0
    for a in range(atoms):
        inner = lane - a * pad
        place = jnp.where((inner >= 0) & (inner < rows(a)), start + inner, place)
        start = start + rows(a)
    packed = lax.broadcasted_iota(jnp.int32, (count, count), 0)
    return jnp.where(packed == place, 1.0, 0.0).astype(jnp.bfloat16)


def spread_matrix(rows, atoms, pad):
    inner = lax.broadcasted_iota(jnp.int32, (pad, atoms * pad), 0)
    packed = lax.broadcasted_iota(jnp.int32, (pad, atoms * pad), 1)
    parts = []
    start = 0
    for a in range(atoms):
        parts.append(jnp.where((packed == start + inner) & (inner < rows(a)), 1.0, 0.0))
        start = start + rows(a)
    return jnp.concatenate(parts, axis=0).astype(jnp.bfloat16)


def pack_kernel(groups, per, rows_ref, coef_ref, main_ref, spill_ref):
    atoms, pad, band_dev = coef_ref.shape
    n, keep, width = main_ref.shape
    matrix = gather_matrix(lambda a: rows_ref[a], atoms, pad)
    for j in range(n):
        used = max(0, min(width, band_dev - j * width))
        if used:
            value = coef_ref[:, :, j * width : j * width + used].reshape(atoms * pad, used)
            packed = jnp.dot(matrix, value, preferred_element_type=jnp.float32)
            packed = packed.astype(jnp.bfloat16)
            main_ref[j, :, :used] = packed[:keep]
            spill_ref[j, :, :used] = packed[keep:]
        if used < width:
            main_ref[j, :, used:] = jnp.zeros((keep, width - used), jnp.bfloat16)
            spill_ref[j, :, used:] = jnp.zeros((atoms * pad - keep, width - used), jnp.bfloat16)


def unpack_kernel(groups, per, offsets, rows_ref, at_ref, spill_ref, *refs):
    in_refs, (out_ref, values, sems) = refs[: len(offsets)], refs[-3:]
    me = at_ref[0]
    atoms, pad, _ = out_ref.shape
    matrix = spread_matrix(lambda a: rows_ref[a], atoms, pad)
    whole, rest = groups // per, groups % per * lanes
    copies = []
    for index, in_ref in enumerate(in_refs):
        peer = me ^ offsets[index]
        packed = jnp.concatenate([in_ref[...], spill_ref[peer]], axis=0)
        value = jnp.dot(matrix, packed, preferred_element_type=jnp.float32)
        values[index] = value.reshape(values.shape[1:])
        start = pl.multiple_of(peer * (per * lanes), lanes)
        for used, there in ((per * lanes, peer < whole), (rest, peer == whole)):
            if used:
                target = out_ref.at[:, :, pl.ds(jnp.where(there, start, 0), used)]
                copy = pltpu.make_async_copy(
                    values.at[index, :, :, :used], target, sems.at[index]
                )
                copies.append((there, copy))
                pl.when(there)(copy.start)
    for there, copy in copies:
        pl.when(there)(copy.wait)


def prep_kernel(piece, at_ref, touch_ref, rows_ref, outer_ref, basis_ref, out_ref, meta, sem):
    beta = at_ref[1]
    tiles_dev, touch_len = touch_ref.shape
    atoms = rows_ref.shape[1]
    start = pl.multiple_of(beta * piece, piece)
    copy = pltpu.make_async_copy(basis_ref.at[pl.ds(start, piece)], out_ref.at[:piece], sem)
    copy.start()
    meta[...] = jnp.zeros_like(meta)
    rest = outer_ref[...]
    for part in range(3):
        rounded = rest.astype(jnp.bfloat16).astype(jnp.float32)
        meta[part * tiles_dev : (part + 1) * tiles_dev, :] = rounded
        rest = rest - rounded
    ids = touch_ref[...]
    row = 3 * tiles_dev
    meta[row : row + tiles_dev, :touch_len] = (ids & 255).astype(jnp.float32)
    row += tiles_dev
    meta[row : row + tiles_dev, :touch_len] = (ids >> 8).astype(jnp.float32)
    row += tiles_dev
    meta[row : row + 1, :atoms] = rows_ref[...].astype(jnp.float32)
    out_ref[piece:] = meta[...].astype(jnp.bfloat16)
    copy.wait()


def weights_kernel(groups, at_ref, weight_ref, after_ref, across_ref, down_ref):
    per = across_ref.shape[1] // lanes
    for q in range(per):
        k = at_ref[0] * per + q
        start = pl.multiple_of(jnp.minimum(k, groups - 1) * lanes, lanes)
        value = jnp.where(k < groups, weight_ref[:, pl.ds(start, lanes)], 0.0)
        across_ref[:, q * lanes : (q + 1) * lanes] = value
        down_ref[q * lanes : (q + 1) * lanes, :] = jnp.broadcast_to(value, (lanes, lanes)).T


def tables_kernel(piece, tiles_dev, touch_len, keep, *refs):
    in_refs, outs = refs[:-6], refs[-6:]
    outer_ref, touch_ref, rows_ref, more_ref, raw, sems = outs
    low = len(in_refs) // 2
    copies = []
    for d in range(raw.shape[0]):
        y, k = d % low, d // low
        source = in_refs[2 * y + (k > 0)].at[max(k - 1, 0), piece:]
        copies.append(pltpu.make_async_copy(source, raw.at[d], sems.at[d]))
    for copy in copies:
        copy.start()
    for copy in copies:
        copy.wait()
    most = jnp.zeros((1, 1), jnp.float32)
    for d in range(raw.shape[0]):
        value = raw[d].astype(jnp.float32)
        span = slice(d * tiles_dev, (d + 1) * tiles_dev)
        parts = [value[p * tiles_dev : (p + 1) * tiles_dev] for p in range(5)]
        outer_ref[span, :] = parts[0] + parts[1] + parts[2]
        touch_ref[span, :] = (parts[3] + 256.0 * parts[4])[:, :touch_len].astype(jnp.int32)
        counts = value[5 * tiles_dev : 5 * tiles_dev + 1, : rows_ref.shape[1]]
        rows_ref[d : d + 1, :] = counts.astype(jnp.int32)
        most = jnp.maximum(most, jnp.sum(counts, axis=1, keepdims=True))
    more_ref[...] = (most > keep).astype(jnp.int32)


def load_basis(basis_refs, basis, sems):
    m = basis.shape[1]
    copies = []
    for index, ref in enumerate(basis_refs):
        part, y, e = index % 2, index // 2 // m, index // 2 % m
        target = basis.at[y, e, part : part + ref.shape[0]]
        copies.append(pltpu.make_async_copy(ref, target, sems.at[index]))
    for copy in copies:
        copy.start()
    return copies


def tile_blocks(touch_ref, index, blocks):
    atoms, touch_len = blocks.shape[1], touch_ref.shape[1]
    ids = [touch_ref[index, s] for s in range(touch_len)]
    return jnp.concatenate([blocks[a // atoms, a % atoms] for a in ids], axis=0)


def tile_basis(beta, index, first, tiles_dev, piece, basis):
    width, m = basis.shape[:2]
    slot, column = index % tiles_dev, index // tiles_dev
    y, k = column % width, column // width
    count = m // tiles_dev
    parts = [basis[y, (slot * count + c) ^ beta, k, :piece] for c in range(count)]
    return jnp.concatenate(parts, axis=0), y, k, slot


def forward_kernel(plan, piece, scale, touch_ref, rows_ref, at_ref, weight_ref, *refs):
    n, k, low, tiles_dev, first = plan
    me, beta = at_ref[0], at_ref[1]
    if first:
        before_ref, block_ref, basis_refs = refs[0], refs[1], refs[2 : 2 + k]
        out_ref, blocks, basis, sems = refs[2 + k :]
    else:
        received, basis_refs = refs[:-4][: -k], refs[:-4][-k:]
        out_ref, blocks, basis, sems = refs[-4:]
    _, atoms, pad, width = blocks.shape
    copies = load_basis(basis_refs, basis, sems)
    if first:
        copies.append(pltpu.make_async_copy(block_ref, blocks, sems.at[k]))
        copies[-1].start()
        out_ref[...] = before_ref[...]
    else:
        for d in range(n):
            owner = me ^ d
            matrix = spread_matrix(lambda a: rows_ref[d, a], atoms, pad)
            packed = jnp.concatenate([ref[owner] for ref in received], axis=0)
            matrix = matrix[:, : packed.shape[0]]
            value = jnp.dot(matrix, packed, preferred_element_type=jnp.float32)
            blocks[owner] = value.astype(jnp.bfloat16).reshape(atoms, pad, width)
        out_ref[...] = jnp.zeros_like(out_ref)
    for copy in copies:
        copy.wait()

    def step(index, carry):
        values, y, z, slot = tile_basis(beta, index, first, tiles_dev, piece, basis)
        d = z * low + first + y
        part = tile_blocks(touch_ref, d * tiles_dev + slot, blocks)
        product = lax.dot_general(
            part, values, (((0,), (0,)), ((), ())), preferred_element_type=jnp.float32
        )
        orbital = product.astype(jnp.bfloat16).astype(jnp.float32)
        weight = jnp.concatenate([weight_ref[...]] * (orbital.shape[1] // lanes), axis=1)
        out_ref[pl.ds((d ^ me) * tiles_dev + slot, 1), :] = scale * jnp.sum(
            weight * orbital * orbital, axis=0, keepdims=True
        )
        return carry

    lax.fori_loop(0, basis.shape[0] * basis.shape[2] * tiles_dev, step, 0, unroll=4)


def backward_kernel(
    n, k, tiles_dev, piece, touch_ref, rows_ref, at_ref, weight_ref, outer_ref, local_ref, *refs
):
    basis_refs, block_ref = refs[:k], refs[k]
    out_refs = refs[k + 1 : k + 1 + n]
    spill_ref, blocks, basis, total, sems = refs[k + 1 + n :]
    me, beta = at_ref[0], at_ref[1]
    tile_count, touch_len = touch_ref.shape
    _, atoms, pad, width = blocks.shape
    copies = load_basis(basis_refs, basis, sems)
    copies.append(pltpu.make_async_copy(block_ref, blocks, sems.at[k]))
    copies[-1].start()
    total[...] = jnp.zeros_like(total)
    weight = weight_ref[...]
    for copy in copies:
        copy.wait()

    def step(index, carry):
        values, y, z, slot = tile_basis(beta, index, 0, tiles_dev, piece, basis)
        d = z * basis.shape[0] + y
        row = d * tiles_dev + slot
        part = tile_blocks(touch_ref, row, blocks)
        potential = (
            outer_ref[pl.ds(row, 1), :] + local_ref[pl.ds((d ^ me) * tiles_dev + slot, 1), :]
        )
        scaled = (values.astype(jnp.float32) * potential).astype(jnp.bfloat16)
        couple = lax.dot_general(
            scaled, values, (((1,), (1,)), ((), ())), preferred_element_type=jnp.float32
        )
        high = couple.astype(jnp.bfloat16)
        low = (couple - high.astype(jnp.float32)).astype(jnp.bfloat16)
        product = jnp.dot(high, part, preferred_element_type=jnp.float32) + jnp.dot(
            low, part, preferred_element_type=jnp.float32
        )
        for s in range(touch_len):
            total[touch_ref[row, s]] += product[s * pad : (s + 1) * pad]
        return carry

    lax.fori_loop(0, tile_count, step, 0, unroll=4)
    for d, out_ref in enumerate(out_refs):
        owner = me ^ d
        matrix = gather_matrix(lambda a: rows_ref[d, a], atoms, pad)
        value = total[pl.ds(owner * atoms, atoms)].reshape(atoms * pad, width)
        value = (weight * value).astype(jnp.bfloat16)
        packed = jnp.dot(matrix, value, preferred_element_type=jnp.float32).astype(jnp.bfloat16)
        out_ref[...] = packed[: out_ref.shape[0]]
        spill_ref[owner] = packed[out_ref.shape[0] :]


smem = pl.BlockSpec(memory_space=pltpu.SMEM)
vmem = pl.BlockSpec(memory_space=pltpu.VMEM)
anywhere = pl.BlockSpec(memory_space=pl.ANY)


def swap(value, axis, offset):
    size = lax.axis_size(axis)
    return lax.ppermute(value, axis, [(i, i ^ offset) for i in range(size)])


def exchange(parts):
    return [parts[0]] + [swap(parts[d], "grid", d) for d in range(1, len(parts))]


def all_sum(value):
    for axis in ("band", "grid"):
        offset = 1
        while offset < lax.axis_size(axis):
            value = value + swap(value, axis, offset)
            offset *= 2
    return value


def body(coefficients, block_rows, touch_atoms, basis_values, outer_field, occupations):
    n = lax.axis_size("grid")
    m = lax.axis_size("band")
    me = lax.axis_index("grid").astype(jnp.int32)
    beta = lax.axis_index("band").astype(jnp.int32)
    atoms, pad, band_dev = coefficients.shape
    tiles_dev, touch_len = touch_atoms.shape
    points = basis_values.shape[2]
    slots = basis_values.shape[1]
    tile_count = tiles_dev * n
    groups = band_dev // lanes
    per = (groups + n - 1) // n
    width = per * lanes
    params = pltpu.CompilerParams(vmem_limit_bytes=big_vmem)
    at = jnp.stack([me, beta])

    keep = atoms * pad * 13 // 16

    def across(value):
        return lax.all_to_all(value, "grid", split_axis=0, concat_axis=0, tiled=True)

    piece = tiles_dev * slots // m
    extra = -(-(5 * tiles_dev + 1) // 16) * 16
    low = 1 << ((n.bit_length() - 1) // 2)
    message = pl.pallas_call(
        functools.partial(prep_kernel, piece),
        out_shape=jax.ShapeDtypeStruct((piece + extra, points), jnp.bfloat16),
        in_specs=[smem, vmem, vmem, vmem, anywhere],
        out_specs=vmem,
        scratch_shapes=[pltpu.VMEM((extra, points), jnp.float32), pltpu.SemaphoreType.DMA],
        compiler_params=params,
        name="prep",
    )(
        at,
        touch_atoms,
        block_rows.reshape(1, atoms),
        outer_field,
        basis_values.reshape(tiles_dev * slots, points),
    )
    size = n // low
    pieces = {}

    def widen(h):
        for y in range(1, low):
            pieces[y, 0, h] = swap(pieces[0, 0, h], "grid", y)

    column = [message] + [swap(message, "grid", low * k) for k in range(1, size)]
    pieces[0, 0, 0] = message[None]
    widen(0)
    sent, spill = pl.pallas_call(
        functools.partial(pack_kernel, groups, per),
        out_shape=[
            jax.ShapeDtypeStruct((n, keep, width), jnp.bfloat16),
            jax.ShapeDtypeStruct((n, atoms * pad - keep, width), jnp.bfloat16),
        ],
        in_specs=[smem, vmem],
        out_specs=[vmem, vmem],
        compiler_params=params,
        name="pack",
    )(block_rows, coefficients)
    sent, spill, column, pieces = lax.optimization_barrier((sent, spill, column, pieces))
    got = across(sent)
    parts = [0, 1]
    pieces[0, 0, 1] = jnp.stack(column[1:])
    widen(1)
    cover = pl.CostEstimate(flops=0, bytes_accessed=1 << 27, transcendentals=0)
    weight, weight_down = pl.pallas_call(
        functools.partial(weights_kernel, groups),
        out_shape=[
            jax.ShapeDtypeStruct((1, width), jnp.float32),
            jax.ShapeDtypeStruct((width, lanes), jnp.float32),
        ],
        in_specs=[smem, vmem, anywhere],
        out_specs=[vmem] * 2,
        compiler_params=params,
        cost_estimate=cover,
        name="weights",
    )(at, occupations[None, :], pieces[0, 0, 1])
    last = [(y, x, 1) for y in range(1, low) for x in range(2, m, 2)]
    for h in parts:
        for y in range(low):
            for x in range(2, m, 2):
                if (y, x, h) not in last:
                    pieces[y, x, h] = swap(pieces[y, 0, h], "band", x)
    pieces, weight, weight_down = lax.optimization_barrier((pieces, weight, weight_down))
    for y, x, h in last:
        pieces[y, x, h] = swap(pieces[y, 0, h], "band", x)
    tables = [pieces[y, 0, h] for y in range(low) for h in parts]
    outer, touch, rows, more = pl.pallas_call(
        functools.partial(tables_kernel, piece, tiles_dev, touch_len, keep),
        out_shape=[
            jax.ShapeDtypeStruct((tile_count, points), jnp.float32),
            jax.ShapeDtypeStruct((tile_count, touch_len), jnp.int32),
            jax.ShapeDtypeStruct((n, atoms), jnp.int32),
            jax.ShapeDtypeStruct((1, 1), jnp.int32),
        ],
        in_specs=[anywhere] * len(tables),
        out_specs=[vmem] * 4,
        scratch_shapes=[
            pltpu.VMEM((n, extra, points), jnp.bfloat16),
            pltpu.SemaphoreType.DMA((n,)),
        ],
        compiler_params=params,
        name="tables",
    )(*tables)
    more = more[0, 0] > 0

    def rest(value):
        return lax.cond(more, across, lambda same: same, value)

    for y, x, h in list(pieces):
        if (y, x, h) not in last:
            pieces[y, x + 1, h] = swap(pieces[y, x, h], "band", 1)
    all_bands = band_dev * m
    held = jax.ShapeDtypeStruct((n, atoms, pad, width), jnp.bfloat16)
    value = jax.ShapeDtypeStruct((tile_count, points), jnp.float32)
    near, far = range(1), range(1, low)

    def basis_of(columns):
        return [pieces[y, e, h] for y in columns for e in range(m) for h in parts]

    def forward(columns, inputs):
        arrays = basis_of(columns)
        first = columns[0]
        plan = (n, len(arrays), low, tiles_dev, first)
        room = [
            pltpu.VMEM((len(columns), m, size, piece + extra, points), jnp.bfloat16),
            pltpu.SemaphoreType.DMA((1 + len(arrays),)),
        ]
        places = [vmem, anywhere] if first else [vmem] * len(inputs)
        return pl.pallas_call(
            functools.partial(forward_kernel, plan, piece, 1.0 / all_bands),
            out_shape=value if first else [value, held],
            in_specs=[smem, smem, smem, vmem] + places + [anywhere] * len(arrays),
            out_specs=vmem if first else [vmem, vmem],
            scratch_shapes=[pltpu.VMEM(held.shape, held.dtype)] * (first > 0) + room,
            compiler_params=params,
            cost_estimate=pl.CostEstimate(
                flops=2 * tile_count // low * len(columns) * slots * width * points,
                bytes_accessed=1 << 27,
                transcendentals=0,
            ),
            name="forward",
        )(touch, rows, at, weight_down, *inputs, *arrays)

    partial_value, blocks = forward(near, [got])
    ends, partial_value, blocks = lax.optimization_barrier(
        ([pieces[k] for k in last], partial_value, blocks)
    )
    for (y, x, h), end in zip(last, ends):
        pieces[y, x, h] = end
        pieces[y, x + 1, h] = swap(end, "band", 1)
    partial_value = forward(far, [partial_value, blocks])

    def again(spill, *_):
        once, blocks = forward(near, [got, across(spill)])
        return forward(far, [once, blocks]), blocks

    partial_value, blocks = lax.cond(
        more, again, lambda spill, *same: same, spill, partial_value, blocks
    )
    basis = basis_of(range(low))
    count = len(basis)
    scratch = [
        pltpu.VMEM((n, atoms, pad, width), jnp.bfloat16),
        pltpu.VMEM((low, m, n // low, piece + extra, points), jnp.bfloat16),
    ]
    sems = pltpu.SemaphoreType.DMA((1 + count,))
    density = all_sum(partial_value)
    local = exchange_coef * jnp.cbrt(density)
    *back, spill = pl.pallas_call(
        functools.partial(backward_kernel, n, count, tiles_dev, piece),
        out_shape=[jax.ShapeDtypeStruct((keep, width), jnp.bfloat16)] * n
        + [jax.ShapeDtypeStruct((n, atoms * pad - keep, width), jnp.bfloat16)],
        in_specs=[smem, smem, smem, vmem, vmem, vmem] + [anywhere] * (1 + count),
        out_specs=[vmem] * (n + 1),
        scratch_shapes=scratch + [pltpu.VMEM((n * atoms, pad, width), jnp.float32), sems],
        compiler_params=params,
        name="backward",
    )(touch, rows, at, weight, outer, local, *basis, blocks)
    returned = exchange(back)
    spill = rest(spill)
    gradient = None
    for offsets in (range(n // 2), range(n // 2, n)):
        before = [] if gradient is None else [gradient]
        gradient = pl.pallas_call(
            functools.partial(unpack_kernel, groups, per, tuple(offsets)),
            out_shape=jax.ShapeDtypeStruct((atoms, pad, band_dev), jnp.float32),
            in_specs=[smem, smem] + [vmem] * (1 + len(offsets)) + [anywhere] * len(before),
            out_specs=anywhere,
            scratch_shapes=[
                pltpu.VMEM((len(offsets), atoms, pad, width), jnp.float32),
                pltpu.SemaphoreType.DMA((len(offsets),)),
            ],
            input_output_aliases={3 + len(offsets): 0} if before else {},
            compiler_params=params,
            cost_estimate=pl.CostEstimate(flops=0, bytes_accessed=1 << 22, transcendentals=0),
            name="unpack",
        )(block_rows, at, spill, *[returned[d] for d in offsets], *before)
    own_density = lax.dynamic_slice_in_dim(density, me * tiles_dev, tiles_dev, 0)
    return (gradient, own_density)


def solution(mesh):
    placed = (
        P("grid", None, "band"),
        P("grid"),
        P("grid", None),
        P("grid", None, None),
        P("grid", None),
        P("band"),
    )
    return jax.shard_map(
        body,
        mesh=mesh,
        in_specs=placed,
        out_specs=(P("grid", None, "band"), P("grid", None)),
        check_vma=False,
    )
```

```python
import functools

import jax
import jax.numpy as jnp
from jax import lax
from jax.experimental import pallas as pl
from jax.experimental.pallas import tpu as pltpu
from jax.sharding import PartitionSpec as P

exchange_coef = -0.9847450218426965
lanes = 128
big_vmem = 60 * 1024 * 1024


def gather_matrix(rows, atoms, pad):
    count = atoms * pad
    lane = lax.broadcasted_iota(jnp.int32, (1, count), 1)
    place = jnp.full((1, count), -1, jnp.int32)
    start = 0
    for a in range(atoms):
        inner = lane - a * pad
        place = jnp.where((inner >= 0) & (inner < rows(a)), start + inner, place)
        start = start + rows(a)
    packed = lax.broadcasted_iota(jnp.int32, (count, count), 0)
    return jnp.where(packed == place, 1.0, 0.0).astype(jnp.bfloat16)


def spread_matrix(rows, atoms, pad):
    inner = lax.broadcasted_iota(jnp.int32, (pad, atoms * pad), 0)
    packed = lax.broadcasted_iota(jnp.int32, (pad, atoms * pad), 1)
    parts = []
    start = 0
    for a in range(atoms):
        parts.append(jnp.where((packed == start + inner) & (inner < rows(a)), 1.0, 0.0))
        start = start + rows(a)
    return jnp.concatenate(parts, axis=0).astype(jnp.bfloat16)


def pack_kernel(groups, per, rows_ref, coef_ref, main_ref, spill_ref):
    atoms, pad, band_dev = coef_ref.shape
    n, keep, width = main_ref.shape
    matrix = gather_matrix(lambda a: rows_ref[a], atoms, pad)
    for j in range(n):
        used = max(0, min(width, band_dev - j * width))
        if used:
            value = coef_ref[:, :, j * width : j * width + used].reshape(atoms * pad, used)
            packed = jnp.dot(matrix, value, preferred_element_type=jnp.float32)
            packed = packed.astype(jnp.bfloat16)
            main_ref[j, :, :used] = packed[:keep]
            spill_ref[j, :, :used] = packed[keep:]
        if used < width:
            main_ref[j, :, used:] = jnp.zeros((keep, width - used), jnp.bfloat16)
            spill_ref[j, :, used:] = jnp.zeros((atoms * pad - keep, width - used), jnp.bfloat16)


def unpack_kernel(groups, per, offsets, rows_ref, at_ref, spill_ref, *refs):
    in_refs, (out_ref, values, sems) = refs[: len(offsets)], refs[-3:]
    me = at_ref[0]
    atoms, pad, _ = out_ref.shape
    matrix = spread_matrix(lambda a: rows_ref[a], atoms, pad)
    whole, rest = groups // per, groups % per * lanes
    copies = []
    for index, in_ref in enumerate(in_refs):
        peer = me ^ offsets[index]
        packed = jnp.concatenate([in_ref[...], spill_ref[peer]], axis=0)
        value = jnp.dot(matrix, packed, preferred_element_type=jnp.float32)
        values[index] = value.reshape(values.shape[1:])
        start = pl.multiple_of(peer * (per * lanes), lanes)
        for used, there in ((per * lanes, peer < whole), (rest, peer == whole)):
            if used:
                target = out_ref.at[:, :, pl.ds(jnp.where(there, start, 0), used)]
                copy = pltpu.make_async_copy(
                    values.at[index, :, :, :used], target, sems.at[index]
                )
                copies.append((there, copy))
                pl.when(there)(copy.start)
    for there, copy in copies:
        pl.when(there)(copy.wait)


def prep_kernel(piece, at_ref, touch_ref, rows_ref, outer_ref, basis_ref, out_ref, meta, sem):
    beta = at_ref[1]
    tiles_dev, touch_len = touch_ref.shape
    atoms = rows_ref.shape[1]
    start = pl.multiple_of(beta * piece, piece)
    copy = pltpu.make_async_copy(basis_ref.at[pl.ds(start, piece)], out_ref.at[:piece], sem)
    copy.start()
    meta[...] = jnp.zeros_like(meta)
    rest = outer_ref[...]
    for part in range(3):
        rounded = rest.astype(jnp.bfloat16).astype(jnp.float32)
        meta[part * tiles_dev : (part + 1) * tiles_dev, :] = rounded
        rest = rest - rounded
    ids = touch_ref[...]
    row = 3 * tiles_dev
    meta[row : row + tiles_dev, :touch_len] = (ids & 255).astype(jnp.float32)
    row += tiles_dev
    meta[row : row + tiles_dev, :touch_len] = (ids >> 8).astype(jnp.float32)
    row += tiles_dev
    meta[row : row + 1, :atoms] = rows_ref[...].astype(jnp.float32)
    out_ref[piece:] = meta[...].astype(jnp.bfloat16)
    copy.wait()


def weights_kernel(groups, at_ref, weight_ref, after_ref, across_ref, down_ref):
    per = across_ref.shape[1] // lanes
    for q in range(per):
        k = at_ref[0] * per + q
        start = pl.multiple_of(jnp.minimum(k, groups - 1) * lanes, lanes)
        value = jnp.where(k < groups, weight_ref[:, pl.ds(start, lanes)], 0.0)
        across_ref[:, q * lanes : (q + 1) * lanes] = value
        down_ref[q * lanes : (q + 1) * lanes, :] = jnp.broadcast_to(value, (lanes, lanes)).T


def tables_kernel(piece, tiles_dev, touch_len, keep, *refs):
    in_refs, outs = refs[:-6], refs[-6:]
    outer_ref, touch_ref, rows_ref, more_ref, raw, sems = outs
    low = len(in_refs) // 2
    copies = []
    for d in range(raw.shape[0]):
        y, k = d % low, d // low
        source = in_refs[2 * y + (k > 0)].at[max(k - 1, 0), piece:]
        copies.append(pltpu.make_async_copy(source, raw.at[d], sems.at[d]))
    for copy in copies:
        copy.start()
    for copy in copies:
        copy.wait()
    most = jnp.zeros((1, 1), jnp.float32)
    for d in range(raw.shape[0]):
        value = raw[d].astype(jnp.float32)
        span = slice(d * tiles_dev, (d + 1) * tiles_dev)
        parts = [value[p * tiles_dev : (p + 1) * tiles_dev] for p in range(5)]
        outer_ref[span, :] = parts[0] + parts[1] + parts[2]
        touch_ref[span, :] = (parts[3] + 256.0 * parts[4])[:, :touch_len].astype(jnp.int32)
        counts = value[5 * tiles_dev : 5 * tiles_dev + 1, : rows_ref.shape[1]]
        rows_ref[d : d + 1, :] = counts.astype(jnp.int32)
        most = jnp.maximum(most, jnp.sum(counts, axis=1, keepdims=True))
    more_ref[...] = (most > keep).astype(jnp.int32)


def load_basis(basis_refs, basis, sems):
    m = basis.shape[1]
    copies = []
    for index, ref in enumerate(basis_refs):
        part, y, e = index % 2, index // 2 // m, index // 2 % m
        target = basis.at[y, e, part : part + ref.shape[0]]
        copies.append(pltpu.make_async_copy(ref, target, sems.at[index]))
    for copy in copies:
        copy.start()
    return copies


def tile_blocks(touch_ref, index, blocks):
    return jnp.concatenate(
        [blocks[touch_ref[index, s]] for s in range(touch_ref.shape[1])], axis=0
    )


def tile_basis(beta, index, y, tiles_dev, piece, basis):
    m = basis.shape[1]
    slot, k = index % tiles_dev, index // tiles_dev
    count = m // tiles_dev
    parts = [basis[y, (slot * count + c) ^ beta, k, :piece] for c in range(count)]
    return jnp.concatenate(parts, axis=0), y, k, slot


def forward_kernel(plan, piece, scale, touch_ref, rows_ref, at_ref, weight_ref, *refs):
    n, k, low, tiles_dev, first = plan
    me, beta = at_ref[0], at_ref[1]
    if first:
        before_ref, block_ref, basis_refs = refs[0], refs[1], refs[2 : 2 + k]
        out_ref, blocks, basis, sems = refs[2 + k :]
    else:
        received, basis_refs = refs[:-4][: -k], refs[:-4][-k:]
        out_ref, blocks, basis, sems = refs[-4:]
    pad, width = blocks.shape[1:]
    atoms = blocks.shape[0] // n
    copies = load_basis(basis_refs, basis, sems)
    if first:
        copies.append(pltpu.make_async_copy(block_ref, blocks, sems.at[k]))
        copies[-1].start()
        out_ref[...] = before_ref[...]
    else:
        for d in range(n):
            owner = me ^ d
            matrix = spread_matrix(lambda a: rows_ref[d, a], atoms, pad)
            packed = jnp.concatenate([ref[owner] for ref in received], axis=0)
            matrix = matrix[:, : packed.shape[0]]
            value = jnp.dot(matrix, packed, preferred_element_type=jnp.float32)
            value = value.astype(jnp.bfloat16).reshape(atoms, pad, width)
            blocks[pl.ds(owner * atoms, atoms)] = value
        out_ref[...] = jnp.zeros_like(out_ref)
    for copy in copies:
        copy.wait()

    def step(y, index, carry):
        values, _, z, slot = tile_basis(beta, index, y, tiles_dev, piece, basis)
        d = z * low + first + y
        part = tile_blocks(touch_ref, d * tiles_dev + slot, blocks)
        product = lax.dot_general(
            part, values, (((0,), (0,)), ((), ())), preferred_element_type=jnp.float32
        )
        orbital = product.astype(jnp.bfloat16).astype(jnp.float32)
        weight = jnp.concatenate([weight_ref[...]] * (orbital.shape[1] // lanes), axis=1)
        out_ref[pl.ds((d ^ me) * tiles_dev + slot, 1), :] = scale * jnp.sum(
            weight * orbital * orbital, axis=0, keepdims=True
        )
        return carry

    for y in range(basis.shape[0]):
        lax.fori_loop(0, basis.shape[2] * tiles_dev, functools.partial(step, y), 0, unroll=8)


def backward_kernel(
    n, k, tiles_dev, piece, touch_ref, rows_ref, at_ref, weight_ref, outer_ref, local_ref, *refs
):
    basis_refs, block_ref = refs[:k], refs[k]
    out_refs = refs[k + 1 : k + 1 + n]
    spill_ref, blocks, basis, total, sems = refs[k + 1 + n :]
    me, beta = at_ref[0], at_ref[1]
    tile_count, touch_len = touch_ref.shape
    pad, width = blocks.shape[1:]
    atoms = blocks.shape[0] // n
    held = pltpu.make_async_copy(block_ref, blocks, sems.at[k])
    held.start()
    copies = load_basis(basis_refs, basis, sems)
    total[...] = jnp.zeros_like(total)
    weight = weight_ref[...]
    held.wait()

    def step(y, index, carry):
        values, _, z, slot = tile_basis(beta, index, y, tiles_dev, piece, basis)
        d = z * basis.shape[0] + y
        row = d * tiles_dev + slot
        part = tile_blocks(touch_ref, row, blocks)
        potential = (
            outer_ref[pl.ds(row, 1), :] + local_ref[pl.ds((d ^ me) * tiles_dev + slot, 1), :]
        )
        scaled = (values.astype(jnp.float32) * potential).astype(jnp.bfloat16)
        couple = lax.dot_general(
            scaled, values, (((1,), (1,)), ((), ())), preferred_element_type=jnp.float32
        )
        high = couple.astype(jnp.bfloat16)
        low = (couple - high.astype(jnp.float32)).astype(jnp.bfloat16)
        product = jnp.dot(high, part, preferred_element_type=jnp.float32) + jnp.dot(
            low, part, preferred_element_type=jnp.float32
        )
        for s in range(touch_len):
            total[touch_ref[row, s]] += product[s * pad : (s + 1) * pad]
        return carry

    columns, each = basis.shape[0], len(copies) // basis.shape[0]
    for y in range(columns):
        for copy in copies[y * each : (y + 1) * each]:
            copy.wait()
        lax.fori_loop(0, tile_count // columns, functools.partial(step, y), 0, unroll=4)
    for d, out_ref in enumerate(out_refs):
        owner = me ^ d
        matrix = gather_matrix(lambda a: rows_ref[d, a], atoms, pad)
        value = total[pl.ds(owner * atoms, atoms)].reshape(atoms * pad, width)
        value = (weight * value).astype(jnp.bfloat16)
        packed = jnp.dot(matrix, value, preferred_element_type=jnp.float32).astype(jnp.bfloat16)
        out_ref[...] = packed[: out_ref.shape[0]]
        spill_ref[owner] = packed[out_ref.shape[0] :]


smem = pl.BlockSpec(memory_space=pltpu.SMEM)
vmem = pl.BlockSpec(memory_space=pltpu.VMEM)
anywhere = pl.BlockSpec(memory_space=pl.ANY)


def swap(value, axis, offset):
    size = lax.axis_size(axis)
    return lax.ppermute(value, axis, [(i, i ^ offset) for i in range(size)])


def exchange(parts):
    return [parts[0]] + [swap(parts[d], "grid", d) for d in range(1, len(parts))]


def all_sum(value):
    for axis in ("band", "grid"):
        offset = 1
        while offset < lax.axis_size(axis):
            value = value + swap(value, axis, offset)
            offset *= 2
    return value


def body(coefficients, block_rows, touch_atoms, basis_values, outer_field, occupations):
    n = lax.axis_size("grid")
    m = lax.axis_size("band")
    me = lax.axis_index("grid").astype(jnp.int32)
    beta = lax.axis_index("band").astype(jnp.int32)
    atoms, pad, band_dev = coefficients.shape
    tiles_dev, touch_len = touch_atoms.shape
    points = basis_values.shape[2]
    slots = basis_values.shape[1]
    tile_count = tiles_dev * n
    groups = band_dev // lanes
    per = (groups + n - 1) // n
    width = per * lanes
    params = pltpu.CompilerParams(vmem_limit_bytes=big_vmem)
    at = jnp.stack([me, beta])

    keep = atoms * pad * 13 // 16

    def across(value):
        return lax.all_to_all(value, "grid", split_axis=0, concat_axis=0, tiled=True)

    piece = tiles_dev * slots // m
    extra = -(-(5 * tiles_dev + 1) // 16) * 16
    low = 1 << ((n.bit_length() - 1) // 2)
    message = pl.pallas_call(
        functools.partial(prep_kernel, piece),
        out_shape=jax.ShapeDtypeStruct((piece + extra, points), jnp.bfloat16),
        in_specs=[smem, vmem, vmem, vmem, anywhere],
        out_specs=vmem,
        scratch_shapes=[pltpu.VMEM((extra, points), jnp.float32), pltpu.SemaphoreType.DMA],
        compiler_params=params,
        name="prep",
    )(
        at,
        touch_atoms,
        block_rows.reshape(1, atoms),
        outer_field,
        basis_values.reshape(tiles_dev * slots, points),
    )
    size = n // low
    pieces = {}

    def widen(h):
        for y in range(1, low):
            pieces[y, 0, h] = swap(pieces[0, 0, h], "grid", y)

    column = [message] + [swap(message, "grid", low * k) for k in range(1, size)]
    pieces[0, 0, 0] = message[None]
    widen(0)
    sent, spill = pl.pallas_call(
        functools.partial(pack_kernel, groups, per),
        out_shape=[
            jax.ShapeDtypeStruct((n, keep, width), jnp.bfloat16),
            jax.ShapeDtypeStruct((n, atoms * pad - keep, width), jnp.bfloat16),
        ],
        in_specs=[smem, vmem],
        out_specs=[vmem, vmem],
        compiler_params=params,
        name="pack",
    )(block_rows, coefficients)
    sent, spill, column, pieces = lax.optimization_barrier((sent, spill, column, pieces))
    got = across(sent)
    parts = [0, 1]
    pieces[0, 0, 1] = jnp.stack(column[1:])
    widen(1)
    cover = pl.CostEstimate(flops=0, bytes_accessed=1 << 27, transcendentals=0)
    weight, weight_down = pl.pallas_call(
        functools.partial(weights_kernel, groups),
        out_shape=[
            jax.ShapeDtypeStruct((1, width), jnp.float32),
            jax.ShapeDtypeStruct((width, lanes), jnp.float32),
        ],
        in_specs=[smem, vmem, anywhere],
        out_specs=[vmem] * 2,
        compiler_params=params,
        cost_estimate=cover,
        name="weights",
    )(at, occupations[None, :], pieces[0, 0, 1])
    last = [(y, x, 1) for y in range(1, low) for x in range(2, m, 2)]
    for h in parts:
        for y in range(low):
            for x in range(2, m, 2):
                if (y, x, h) not in last:
                    pieces[y, x, h] = swap(pieces[y, 0, h], "band", x)
    pieces, weight, weight_down = lax.optimization_barrier((pieces, weight, weight_down))
    for y, x, h in last:
        pieces[y, x, h] = swap(pieces[y, 0, h], "band", x)
    tables = [pieces[y, 0, h] for y in range(low) for h in parts]
    outer, touch, rows, more = pl.pallas_call(
        functools.partial(tables_kernel, piece, tiles_dev, touch_len, keep),
        out_shape=[
            jax.ShapeDtypeStruct((tile_count, points), jnp.float32),
            jax.ShapeDtypeStruct((tile_count, touch_len), jnp.int32),
            jax.ShapeDtypeStruct((n, atoms), jnp.int32),
            jax.ShapeDtypeStruct((1, 1), jnp.int32),
        ],
        in_specs=[anywhere] * len(tables),
        out_specs=[vmem] * 4,
        scratch_shapes=[
            pltpu.VMEM((n, extra, points), jnp.bfloat16),
            pltpu.SemaphoreType.DMA((n,)),
        ],
        compiler_params=params,
        name="tables",
    )(*tables)
    more = more[0, 0] > 0

    def rest(value):
        return lax.cond(more, across, lambda same: same, value)

    for y, x, h in list(pieces):
        if (y, x, h) not in last:
            pieces[y, x + 1, h] = swap(pieces[y, x, h], "band", 1)
    all_bands = band_dev * m
    held = jax.ShapeDtypeStruct((n * atoms, pad, width), jnp.bfloat16)
    value = jax.ShapeDtypeStruct((tile_count, points), jnp.float32)
    near, far = range(1), range(1, low)

    def basis_of(columns):
        return [pieces[y, e, h] for y in columns for e in range(m) for h in parts]

    def forward(columns, inputs):
        arrays = basis_of(columns)
        first = columns[0]
        plan = (n, len(arrays), low, tiles_dev, first)
        room = [
            pltpu.VMEM((len(columns), m, size, piece + extra, points), jnp.bfloat16),
            pltpu.SemaphoreType.DMA((1 + len(arrays),)),
        ]
        places = [vmem, anywhere] if first else [vmem] * len(inputs)
        return pl.pallas_call(
            functools.partial(forward_kernel, plan, piece, 1.0 / all_bands),
            out_shape=value if first else [value, held],
            in_specs=[smem, smem, smem, vmem] + places + [anywhere] * len(arrays),
            out_specs=vmem if first else [vmem, vmem],
            scratch_shapes=[pltpu.VMEM(held.shape, held.dtype)] * (first > 0) + room,
            compiler_params=params,
            cost_estimate=pl.CostEstimate(
                flops=2 * tile_count // low * len(columns) * slots * width * points,
                bytes_accessed=1 << 27,
                transcendentals=0,
            ),
            name="forward",
        )(touch, rows, at, weight_down, *inputs, *arrays)

    partial_value, blocks = forward(near, [got])
    ends, partial_value, blocks = lax.optimization_barrier(
        ([pieces[k] for k in last], partial_value, blocks)
    )
    for (y, x, h), end in zip(last, ends):
        pieces[y, x, h] = end
        pieces[y, x + 1, h] = swap(end, "band", 1)
    partial_value = forward(far, [partial_value, blocks])

    def again(spill, *_):
        once, blocks = forward(near, [got, across(spill)])
        return forward(far, [once, blocks]), blocks

    partial_value, blocks = lax.cond(
        more, again, lambda spill, *same: same, spill, partial_value, blocks
    )
    basis = basis_of(range(low))
    count = len(basis)
    scratch = [
        pltpu.VMEM((n * atoms, pad, width), jnp.bfloat16),
        pltpu.VMEM((low, m, n // low, piece + extra, points), jnp.bfloat16),
    ]
    sems = pltpu.SemaphoreType.DMA((1 + count,))
    density = all_sum(partial_value)
    local = exchange_coef * jnp.cbrt(density)
    *back, spill = pl.pallas_call(
        functools.partial(backward_kernel, n, count, tiles_dev, piece),
        out_shape=[jax.ShapeDtypeStruct((keep, width), jnp.bfloat16)] * n
        + [jax.ShapeDtypeStruct((n, atoms * pad - keep, width), jnp.bfloat16)],
        in_specs=[smem, smem, smem, vmem, vmem, vmem] + [anywhere] * (1 + count),
        out_specs=[vmem] * (n + 1),
        scratch_shapes=scratch + [pltpu.VMEM((n * atoms, pad, width), jnp.float32), sems],
        compiler_params=params,
        name="backward",
    )(touch, rows, at, weight, outer, local, *basis, blocks)
    returned = exchange(back)
    spill = rest(spill)
    gradient = None
    half = n // 2
    early = [*range(half - 1), *range(half, n - n // 4), half - 1]
    for offsets in (early, range(n - n // 4, n)):
        before = [] if gradient is None else [gradient]
        gradient = pl.pallas_call(
            functools.partial(unpack_kernel, groups, per, tuple(offsets)),
            out_shape=jax.ShapeDtypeStruct((atoms, pad, band_dev), jnp.float32),
            in_specs=[smem, smem] + [vmem] * (1 + len(offsets)) + [anywhere] * len(before),
            out_specs=anywhere,
            scratch_shapes=[
                pltpu.VMEM((len(offsets), atoms, pad, width), jnp.float32),
                pltpu.SemaphoreType.DMA((len(offsets),)),
            ],
            input_output_aliases={3 + len(offsets): 0} if before else {},
            compiler_params=params,
            cost_estimate=pl.CostEstimate(flops=0, bytes_accessed=1 << 22, transcendentals=0),
            name="unpack",
        )(block_rows, at, spill, *[returned[d] for d in offsets], *before)
    own_density = lax.dynamic_slice_in_dim(density, me * tiles_dev, tiles_dev, 0)
    return (gradient, own_density)


def solution(mesh):
    placed = (
        P("grid", None, "band"),
        P("grid"),
        P("grid", None),
        P("grid", None, None),
        P("grid", None),
        P("band"),
    )
    return jax.shard_map(
        body,
        mesh=mesh,
        in_specs=placed,
        out_specs=(P("grid", None, "band"), P("grid", None)),
        check_vma=False,
    )
```

```python
import functools

import jax
import jax.numpy as jnp
from jax import lax
from jax.experimental import pallas as pl
from jax.experimental.pallas import tpu as pltpu
from jax.sharding import PartitionSpec as P

exchange_coef = -0.9847450218426965
lanes = 128
big_vmem = 60 * 1024 * 1024


def gather_matrix(rows, atoms, pad):
    count = atoms * pad
    lane = lax.broadcasted_iota(jnp.int32, (1, count), 1)
    place = jnp.full((1, count), -1, jnp.int32)
    start = 0
    for a in range(atoms):
        inner = lane - a * pad
        place = jnp.where((inner >= 0) & (inner < rows(a)), start + inner, place)
        start = start + rows(a)
    packed = lax.broadcasted_iota(jnp.int32, (count, count), 0)
    return jnp.where(packed == place, 1.0, 0.0).astype(jnp.bfloat16)


def spread_matrix(rows, atoms, pad):
    inner = lax.broadcasted_iota(jnp.int32, (pad, atoms * pad), 0)
    packed = lax.broadcasted_iota(jnp.int32, (pad, atoms * pad), 1)
    parts = []
    start = 0
    for a in range(atoms):
        parts.append(jnp.where((packed == start + inner) & (inner < rows(a)), 1.0, 0.0))
        start = start + rows(a)
    return jnp.concatenate(parts, axis=0).astype(jnp.bfloat16)


def pack_kernel(groups, per, rows_ref, coef_ref, main_ref, spill_ref):
    atoms, pad, band_dev = coef_ref.shape
    n, keep, width = main_ref.shape
    matrix = gather_matrix(lambda a: rows_ref[a], atoms, pad)
    for j in range(n):
        used = max(0, min(width, band_dev - j * width))
        if used:
            value = coef_ref[:, :, j * width : j * width + used].reshape(atoms * pad, used)
            packed = jnp.dot(matrix, value, preferred_element_type=jnp.float32)
            packed = packed.astype(jnp.bfloat16)
            main_ref[j, :, :used] = packed[:keep]
            spill_ref[j, :, :used] = packed[keep:]
        if used < width:
            main_ref[j, :, used:] = jnp.zeros((keep, width - used), jnp.bfloat16)
            spill_ref[j, :, used:] = jnp.zeros((atoms * pad - keep, width - used), jnp.bfloat16)


def unpack_kernel(groups, per, offsets, rows_ref, at_ref, spill_ref, *refs):
    in_refs, (out_ref, values, sems) = refs[: len(offsets)], refs[-3:]
    me = at_ref[0]
    atoms, pad, _ = out_ref.shape
    matrix = spread_matrix(lambda a: rows_ref[a], atoms, pad)
    whole, rest = groups // per, groups % per * lanes
    copies = []
    for index, in_ref in enumerate(in_refs):
        peer = me ^ offsets[index]
        packed = jnp.concatenate([in_ref[...], spill_ref[peer]], axis=0)
        value = jnp.dot(matrix, packed, preferred_element_type=jnp.float32)
        values[index] = value.reshape(values.shape[1:])
        start = pl.multiple_of(peer * (per * lanes), lanes)
        for used, there in ((per * lanes, peer < whole), (rest, peer == whole)):
            if used:
                target = out_ref.at[:, :, pl.ds(jnp.where(there, start, 0), used)]
                copy = pltpu.make_async_copy(
                    values.at[index, :, :, :used], target, sems.at[index]
                )
                copies.append((there, copy))
                pl.when(there)(copy.start)
    for there, copy in copies:
        pl.when(there)(copy.wait)


def prep_kernel(piece, at_ref, touch_ref, rows_ref, outer_ref, basis_ref, out_ref, meta, sem):
    beta = at_ref[1]
    tiles_dev, touch_len = touch_ref.shape
    atoms = rows_ref.shape[1]
    start = pl.multiple_of(beta * piece, piece)
    copy = pltpu.make_async_copy(basis_ref.at[pl.ds(start, piece)], out_ref.at[:piece], sem)
    copy.start()
    meta[...] = jnp.zeros_like(meta)
    rest = outer_ref[...]
    for part in range(3):
        rounded = rest.astype(jnp.bfloat16).astype(jnp.float32)
        meta[part * tiles_dev : (part + 1) * tiles_dev, :] = rounded
        rest = rest - rounded
    ids = touch_ref[...]
    row = 3 * tiles_dev
    meta[row : row + tiles_dev, :touch_len] = (ids & 255).astype(jnp.float32)
    row += tiles_dev
    meta[row : row + tiles_dev, :touch_len] = (ids >> 8).astype(jnp.float32)
    row += tiles_dev
    meta[row : row + 1, :atoms] = rows_ref[...].astype(jnp.float32)
    out_ref[piece:] = meta[...].astype(jnp.bfloat16)
    copy.wait()


def weights_kernel(groups, at_ref, weight_ref, after_ref, across_ref, down_ref):
    per = across_ref.shape[1] // lanes
    for q in range(per):
        k = at_ref[0] * per + q
        start = pl.multiple_of(jnp.minimum(k, groups - 1) * lanes, lanes)
        value = jnp.where(k < groups, weight_ref[:, pl.ds(start, lanes)], 0.0)
        across_ref[:, q * lanes : (q + 1) * lanes] = value
        down_ref[q * lanes : (q + 1) * lanes, :] = jnp.broadcast_to(value, (lanes, lanes)).T


def tables_kernel(piece, tiles_dev, touch_len, keep, *refs):
    in_refs, outs = refs[:-6], refs[-6:]
    outer_ref, touch_ref, rows_ref, more_ref, raw, sems = outs
    low = len(in_refs) // 2
    copies = []
    for d in range(raw.shape[0]):
        y, k = d % low, d // low
        source = in_refs[2 * y + (k > 0)].at[max(k - 1, 0), piece:]
        copies.append(pltpu.make_async_copy(source, raw.at[d], sems.at[d]))
    for copy in copies:
        copy.start()
    for copy in copies:
        copy.wait()
    most = jnp.zeros((1, 1), jnp.float32)
    for d in range(raw.shape[0]):
        value = raw[d].astype(jnp.float32)
        span = slice(d * tiles_dev, (d + 1) * tiles_dev)
        parts = [value[p * tiles_dev : (p + 1) * tiles_dev] for p in range(5)]
        outer_ref[span, :] = parts[0] + parts[1] + parts[2]
        touch_ref[span, :] = (parts[3] + 256.0 * parts[4])[:, :touch_len].astype(jnp.int32)
        counts = value[5 * tiles_dev : 5 * tiles_dev + 1, : rows_ref.shape[1]]
        rows_ref[d : d + 1, :] = counts.astype(jnp.int32)
        most = jnp.maximum(most, jnp.sum(counts, axis=1, keepdims=True))
    more_ref[...] = (most > keep).astype(jnp.int32)


def load_basis(keys, basis_refs, basis, sems):
    copies = []
    for index, ref in enumerate(basis_refs):
        part, (y, e) = index % 2, keys[index // 2]
        target = basis.at[y, e, part : part + ref.shape[0]]
        copies.append(pltpu.make_async_copy(ref, target, sems.at[index]))
    for copy in copies:
        copy.start()
    return copies


def tile_blocks(touch_ref, index, blocks):
    return jnp.concatenate(
        [blocks[touch_ref[index, s]] for s in range(touch_ref.shape[1])], axis=0
    )


def tile_basis(beta, y, k, slot, tiles_dev, piece, basis):
    count = basis.shape[1] // tiles_dev
    parts = [basis[y, (slot * count + c) ^ beta, k, :piece] for c in range(count)]
    return jnp.concatenate(parts, axis=0)


def forward_kernel(plan, piece, scale, touch_ref, rows_ref, at_ref, weight_ref, *refs):
    n, keys, tiles_dev, first = plan
    k = 2 * len(keys)
    me, beta = at_ref[0], at_ref[1]
    if first:
        before_ref, block_ref, basis_refs = refs[0], refs[1], refs[2 : 2 + k]
        out_ref, blocks, basis, sems = refs[2 + k :]
    else:
        received, basis_refs = refs[:-4][: -k], refs[:-4][-k:]
        out_ref, blocks, basis, sems = refs[-4:]
    pad, width = blocks.shape[1:]
    atoms = blocks.shape[0] // n
    copies = load_basis(keys, basis_refs, basis, sems)
    if first:
        copies.append(pltpu.make_async_copy(block_ref, blocks, sems.at[k]))
        copies[-1].start()
        out_ref[...] = before_ref[...]
    else:
        for d in range(n):
            owner = me ^ d
            matrix = spread_matrix(lambda a: rows_ref[d, a], atoms, pad)
            packed = jnp.concatenate([ref[owner] for ref in received], axis=0)
            matrix = matrix[:, : packed.shape[0]]
            value = jnp.dot(matrix, packed, preferred_element_type=jnp.float32)
            value = value.astype(jnp.bfloat16).reshape(atoms, pad, width)
            blocks[pl.ds(owner * atoms, atoms)] = value
        out_ref[...] = jnp.zeros_like(out_ref)
    for copy in copies:
        copy.wait()

    low, m, size = basis.shape[:3]
    own = beta // (m // tiles_dev)

    def step(y, slots, index, carry):
        z, slot = index // len(slots), slots[0]
        if len(slots) > 1:
            slot = slots[0] + index % len(slots)
        slot = (slot + own) % tiles_dev
        values = tile_basis(beta, y, z, slot, tiles_dev, piece, basis)
        d = z * low + y
        part = tile_blocks(touch_ref, d * tiles_dev + slot, blocks)
        product = lax.dot_general(
            part, values, (((0,), (0,)), ((), ())), preferred_element_type=jnp.float32
        )
        orbital = product.astype(jnp.bfloat16).astype(jnp.float32)
        weight = jnp.concatenate([weight_ref[...]] * (orbital.shape[1] // lanes), axis=1)
        out_ref[pl.ds((d ^ me) * tiles_dev + slot, 1), :] = scale * jnp.sum(
            weight * orbital * orbital, axis=0, keepdims=True
        )
        return carry

    for y in range(1 if first else 0, low):
        slots = range(1, tiles_dev) if first else range(tiles_dev if y == 0 else 1)
        if slots:
            lax.fori_loop(
                0, size * len(slots), functools.partial(step, y, slots), 0, unroll=4
            )


def backward_kernel(
    n, k, tiles_dev, piece, touch_ref, rows_ref, at_ref, weight_ref, outer_ref, local_ref, *refs
):
    basis_refs, block_ref = refs[:k], refs[k]
    out_refs = refs[k + 1 : k + 1 + n]
    spill_ref, blocks, basis, total, sems = refs[k + 1 + n :]
    me, beta = at_ref[0], at_ref[1]
    tile_count, touch_len = touch_ref.shape
    pad, width = blocks.shape[1:]
    atoms = blocks.shape[0] // n
    held = pltpu.make_async_copy(block_ref, blocks, sems.at[k])
    held.start()
    keys = [(y, e) for y in range(basis.shape[0]) for e in range(basis.shape[1])]
    copies = load_basis(keys, basis_refs, basis, sems)
    total[...] = jnp.zeros_like(total)
    weight = weight_ref[...]
    held.wait()

    def step(y, index, carry):
        z, slot = index // tiles_dev, index % tiles_dev
        values = tile_basis(beta, y, z, slot, tiles_dev, piece, basis)
        d = z * basis.shape[0] + y
        row = d * tiles_dev + slot
        part = tile_blocks(touch_ref, row, blocks)
        potential = (
            outer_ref[pl.ds(row, 1), :] + local_ref[pl.ds((d ^ me) * tiles_dev + slot, 1), :]
        )
        scaled = (values.astype(jnp.float32) * potential).astype(jnp.bfloat16)
        couple = lax.dot_general(
            scaled, values, (((1,), (1,)), ((), ())), preferred_element_type=jnp.float32
        )
        high = couple.astype(jnp.bfloat16)
        low = (couple - high.astype(jnp.float32)).astype(jnp.bfloat16)
        product = jnp.dot(high, part, preferred_element_type=jnp.float32) + jnp.dot(
            low, part, preferred_element_type=jnp.float32
        )
        for s in range(touch_len):
            total[touch_ref[row, s]] += product[s * pad : (s + 1) * pad]
        return carry

    columns, each = basis.shape[0], len(copies) // basis.shape[0]
    for y in range(columns):
        for copy in copies[y * each : (y + 1) * each]:
            copy.wait()
        lax.fori_loop(0, tile_count // columns, functools.partial(step, y), 0, unroll=8)
    for d, out_ref in enumerate(out_refs):
        owner = me ^ d
        matrix = gather_matrix(lambda a: rows_ref[d, a], atoms, pad)
        value = total[pl.ds(owner * atoms, atoms)].reshape(atoms * pad, width)
        value = (weight * value).astype(jnp.bfloat16)
        packed = jnp.dot(matrix, value, preferred_element_type=jnp.float32).astype(jnp.bfloat16)
        out_ref[...] = packed[: out_ref.shape[0]]
        spill_ref[owner] = packed[out_ref.shape[0] :]


smem = pl.BlockSpec(memory_space=pltpu.SMEM)
vmem = pl.BlockSpec(memory_space=pltpu.VMEM)
anywhere = pl.BlockSpec(memory_space=pl.ANY)


def swap(value, axis, offset):
    size = lax.axis_size(axis)
    return lax.ppermute(value, axis, [(i, i ^ offset) for i in range(size)])


def exchange(parts):
    return [parts[0]] + [swap(parts[d], "grid", d) for d in range(1, len(parts))]


def all_sum(value):
    for axis in ("band", "grid"):
        offset = 1
        while offset < lax.axis_size(axis):
            value = value + swap(value, axis, offset)
            offset *= 2
    return value


def body(coefficients, block_rows, touch_atoms, basis_values, outer_field, occupations):
    n = lax.axis_size("grid")
    m = lax.axis_size("band")
    me = lax.axis_index("grid").astype(jnp.int32)
    beta = lax.axis_index("band").astype(jnp.int32)
    atoms, pad, band_dev = coefficients.shape
    tiles_dev, touch_len = touch_atoms.shape
    points = basis_values.shape[2]
    slots = basis_values.shape[1]
    tile_count = tiles_dev * n
    groups = band_dev // lanes
    per = (groups + n - 1) // n
    width = per * lanes
    params = pltpu.CompilerParams(vmem_limit_bytes=big_vmem)
    at = jnp.stack([me, beta])

    keep = atoms * pad * 13 // 16

    def across(value):
        return lax.all_to_all(value, "grid", split_axis=0, concat_axis=0, tiled=True)

    piece = tiles_dev * slots // m
    extra = -(-(5 * tiles_dev + 1) // 16) * 16
    low = 1 << ((n.bit_length() - 1) // 2)
    message = pl.pallas_call(
        functools.partial(prep_kernel, piece),
        out_shape=jax.ShapeDtypeStruct((piece + extra, points), jnp.bfloat16),
        in_specs=[smem, vmem, vmem, vmem, anywhere],
        out_specs=vmem,
        scratch_shapes=[pltpu.VMEM((extra, points), jnp.float32), pltpu.SemaphoreType.DMA],
        compiler_params=params,
        name="prep",
    )(
        at,
        touch_atoms,
        block_rows.reshape(1, atoms),
        outer_field,
        basis_values.reshape(tiles_dev * slots, points),
    )
    size = n // low
    pieces = {}

    def widen(h):
        for y in range(1, low):
            pieces[y, 0, h] = swap(pieces[0, 0, h], "grid", y)

    column = [message] + [swap(message, "grid", low * k) for k in range(1, size)]
    pieces[0, 0, 0] = message[None]
    widen(0)
    sent, spill = pl.pallas_call(
        functools.partial(pack_kernel, groups, per),
        out_shape=[
            jax.ShapeDtypeStruct((n, keep, width), jnp.bfloat16),
            jax.ShapeDtypeStruct((n, atoms * pad - keep, width), jnp.bfloat16),
        ],
        in_specs=[smem, vmem],
        out_specs=[vmem, vmem],
        compiler_params=params,
        name="pack",
    )(block_rows, coefficients)
    sent, spill, column, pieces = lax.optimization_barrier((sent, spill, column, pieces))
    got = across(sent)
    parts = [0, 1]
    pieces[0, 0, 1] = jnp.stack(column[1:])
    widen(1)
    cover = pl.CostEstimate(flops=0, bytes_accessed=1 << 27, transcendentals=0)
    weight, weight_down = pl.pallas_call(
        functools.partial(weights_kernel, groups),
        out_shape=[
            jax.ShapeDtypeStruct((1, width), jnp.float32),
            jax.ShapeDtypeStruct((width, lanes), jnp.float32),
        ],
        in_specs=[smem, vmem, anywhere],
        out_specs=[vmem] * 2,
        compiler_params=params,
        cost_estimate=cover,
        name="weights",
    )(at, occupations[None, :], pieces[0, 0, 1])
    count = m // tiles_dev
    last = [(y, x, 1) for y in range(1, low) for x in range(max(2, count), m, 2)]
    for h in parts:
        for y in range(low):
            for x in range(2, m, 2):
                if (y, x, h) not in last:
                    pieces[y, x, h] = swap(pieces[y, 0, h], "band", x)
    pieces, weight, weight_down = lax.optimization_barrier((pieces, weight, weight_down))
    for y, x, h in last:
        pieces[y, x, h] = swap(pieces[y, 0, h], "band", x)
    tables = [pieces[y, 0, h] for y in range(low) for h in parts]
    outer, touch, rows, more = pl.pallas_call(
        functools.partial(tables_kernel, piece, tiles_dev, touch_len, keep),
        out_shape=[
            jax.ShapeDtypeStruct((tile_count, points), jnp.float32),
            jax.ShapeDtypeStruct((tile_count, touch_len), jnp.int32),
            jax.ShapeDtypeStruct((n, atoms), jnp.int32),
            jax.ShapeDtypeStruct((1, 1), jnp.int32),
        ],
        in_specs=[anywhere] * len(tables),
        out_specs=[vmem] * 4,
        scratch_shapes=[
            pltpu.VMEM((n, extra, points), jnp.bfloat16),
            pltpu.SemaphoreType.DMA((n,)),
        ],
        compiler_params=params,
        name="tables",
    )(*tables)
    more = more[0, 0] > 0

    def rest(value):
        return lax.cond(more, across, lambda same: same, value)

    for y, x, h in list(pieces):
        if (y, x, h) not in last:
            pieces[y, x + 1, h] = swap(pieces[y, x, h], "band", 1)
    all_bands = band_dev * m
    held = jax.ShapeDtypeStruct((n * atoms, pad, width), jnp.bfloat16)
    value = jax.ShapeDtypeStruct((tile_count, points), jnp.float32)
    every = [(y, e) for y in range(low) for e in range(m)]
    far = [(y, e) for y, e in every if y > 0 and e >= count]
    near = [key for key in every if key not in far]

    def basis_of(keys):
        return [pieces[y, e, h] for y, e in keys for h in parts]

    def forward(keys, inputs):
        arrays = basis_of(keys)
        first = keys is far
        plan = (n, keys, tiles_dev, first)
        room = [
            pltpu.VMEM((low, m, size, piece + extra, points), jnp.bfloat16),
            pltpu.SemaphoreType.DMA((1 + len(arrays),)),
        ]
        places = [vmem, anywhere] if first else [vmem] * len(inputs)
        return pl.pallas_call(
            functools.partial(forward_kernel, plan, piece, 1.0 / all_bands),
            out_shape=value if first else [value, held],
            in_specs=[smem, smem, smem, vmem] + places + [anywhere] * len(arrays),
            out_specs=vmem if first else [vmem, vmem],
            scratch_shapes=[pltpu.VMEM(held.shape, held.dtype)] * first + room,
            compiler_params=params,
            cost_estimate=pl.CostEstimate(
                flops=2 * tile_count * len(keys) // len(every) * slots * width * points,
                bytes_accessed=1 << 27,
                transcendentals=0,
            ),
            name="forward",
        )(touch, rows, at, weight_down, *inputs, *arrays)

    partial_value, blocks = forward(near, [got])
    ends, partial_value, blocks = lax.optimization_barrier(
        ([pieces[k] for k in last], partial_value, blocks)
    )
    for (y, x, h), end in zip(last, ends):
        pieces[y, x, h] = end
        pieces[y, x + 1, h] = swap(end, "band", 1)
    partial_value = forward(far, [partial_value, blocks])

    def again(spill, *_):
        once, blocks = forward(near, [got, across(spill)])
        return forward(far, [once, blocks]), blocks

    partial_value, blocks = lax.cond(
        more, again, lambda spill, *same: same, spill, partial_value, blocks
    )
    basis = basis_of(every)
    count = len(basis)
    scratch = [
        pltpu.VMEM((n * atoms, pad, width), jnp.bfloat16),
        pltpu.VMEM((low, m, n // low, piece + extra, points), jnp.bfloat16),
    ]
    sems = pltpu.SemaphoreType.DMA((1 + count,))
    density = all_sum(partial_value)
    local = exchange_coef * jnp.cbrt(density)
    *back, spill = pl.pallas_call(
        functools.partial(backward_kernel, n, count, tiles_dev, piece),
        out_shape=[jax.ShapeDtypeStruct((keep, width), jnp.bfloat16)] * n
        + [jax.ShapeDtypeStruct((n, atoms * pad - keep, width), jnp.bfloat16)],
        in_specs=[smem, smem, smem, vmem, vmem, vmem] + [anywhere] * (1 + count),
        out_specs=[vmem] * (n + 1),
        scratch_shapes=scratch + [pltpu.VMEM((n * atoms, pad, width), jnp.float32), sems],
        compiler_params=params,
        name="backward",
    )(touch, rows, at, weight, outer, local, *basis, blocks)
    returned = exchange(back)
    spill = rest(spill)
    gradient = None
    half = n // 2
    early = [*range(half - 1), *range(half, n - n // 4), half - 1]
    for offsets in (early, range(n - n // 4, n)):
        before = [] if gradient is None else [gradient]
        gradient = pl.pallas_call(
            functools.partial(unpack_kernel, groups, per, tuple(offsets)),
            out_shape=jax.ShapeDtypeStruct((atoms, pad, band_dev), jnp.float32),
            in_specs=[smem, smem] + [vmem] * (1 + len(offsets)) + [anywhere] * len(before),
            out_specs=anywhere,
            scratch_shapes=[
                pltpu.VMEM((len(offsets), atoms, pad, width), jnp.float32),
                pltpu.SemaphoreType.DMA((len(offsets),)),
            ],
            input_output_aliases={3 + len(offsets): 0} if before else {},
            compiler_params=params,
            cost_estimate=pl.CostEstimate(flops=0, bytes_accessed=1 << 22, transcendentals=0),
            name="unpack",
        )(block_rows, at, spill, *[returned[d] for d in offsets], *before)
    own_density = lax.dynamic_slice_in_dim(density, me * tiles_dev, tiles_dev, 0)
    return (gradient, own_density)


def solution(mesh):
    placed = (
        P("grid", None, "band"),
        P("grid"),
        P("grid", None),
        P("grid", None, None),
        P("grid", None),
        P("band"),
    )
    return jax.shard_map(
        body,
        mesh=mesh,
        in_specs=placed,
        out_specs=(P("grid", None, "band"), P("grid", None)),
        check_vma=False,
    )
```

```python
import functools

import jax
import jax.numpy as jnp
from jax import lax
from jax.experimental import pallas as pl
from jax.experimental.pallas import tpu as pltpu
from jax.sharding import PartitionSpec as P

exchange_coef = -0.9847450218426965
lanes = 128
big_vmem = 60 * 1024 * 1024


def gather_matrix(rows, atoms, pad):
    count = atoms * pad
    lane = lax.broadcasted_iota(jnp.int32, (1, count), 1)
    place = jnp.full((1, count), -1, jnp.int32)
    start = 0
    for a in range(atoms):
        inner = lane - a * pad
        place = jnp.where((inner >= 0) & (inner < rows(a)), start + inner, place)
        start = start + rows(a)
    packed = lax.broadcasted_iota(jnp.int32, (count, count), 0)
    return jnp.where(packed == place, 1.0, 0.0).astype(jnp.bfloat16)


def spread_matrix(rows, atoms, pad):
    inner = lax.broadcasted_iota(jnp.int32, (pad, atoms * pad), 0)
    packed = lax.broadcasted_iota(jnp.int32, (pad, atoms * pad), 1)
    parts = []
    start = 0
    for a in range(atoms):
        parts.append(jnp.where((packed == start + inner) & (inner < rows(a)), 1.0, 0.0))
        start = start + rows(a)
    return jnp.concatenate(parts, axis=0).astype(jnp.bfloat16)


def pack_kernel(groups, per, rows_ref, coef_ref, main_ref, spill_ref):
    atoms, pad, band_dev = coef_ref.shape
    n, keep, width = main_ref.shape
    matrix = gather_matrix(lambda a: rows_ref[a], atoms, pad)
    for j in range(n):
        used = max(0, min(width, band_dev - j * width))
        if used:
            value = coef_ref[:, :, j * width : j * width + used].reshape(atoms * pad, used)
            packed = jnp.dot(matrix, value, preferred_element_type=jnp.float32)
            packed = packed.astype(jnp.bfloat16)
            main_ref[j, :, :used] = packed[:keep]
            spill_ref[j, :, :used] = packed[keep:]
        if used < width:
            main_ref[j, :, used:] = jnp.zeros((keep, width - used), jnp.bfloat16)
            spill_ref[j, :, used:] = jnp.zeros((atoms * pad - keep, width - used), jnp.bfloat16)


def unpack_kernel(groups, per, offsets, rows_ref, at_ref, spill_ref, *refs):
    in_refs, (out_ref, values, sems) = refs[: len(offsets)], refs[-3:]
    me = at_ref[0]
    atoms, pad, _ = out_ref.shape
    matrix = spread_matrix(lambda a: rows_ref[a], atoms, pad)
    whole, rest = groups // per, groups % per * lanes
    copies = []
    for index, in_ref in enumerate(in_refs):
        peer = me ^ offsets[index]
        packed = jnp.concatenate([in_ref[...], spill_ref[peer]], axis=0)
        value = jnp.dot(matrix, packed, preferred_element_type=jnp.float32)
        values[index] = value.reshape(values.shape[1:])
        start = pl.multiple_of(peer * (per * lanes), lanes)
        for used, there in ((per * lanes, peer < whole), (rest, peer == whole)):
            if used:
                target = out_ref.at[:, :, pl.ds(jnp.where(there, start, 0), used)]
                copy = pltpu.make_async_copy(
                    values.at[index, :, :, :used], target, sems.at[index]
                )
                copies.append((there, copy))
                pl.when(there)(copy.start)
    for there, copy in copies:
        pl.when(there)(copy.wait)


def prep_kernel(piece, at_ref, touch_ref, rows_ref, outer_ref, basis_ref, out_ref, meta, sem):
    beta = at_ref[1]
    tiles_dev, touch_len = touch_ref.shape
    atoms = rows_ref.shape[1]
    start = pl.multiple_of(beta * piece, piece)
    copy = pltpu.make_async_copy(basis_ref.at[pl.ds(start, piece)], out_ref.at[:piece], sem)
    copy.start()
    meta[...] = jnp.zeros_like(meta)
    rest = outer_ref[...]
    for part in range(3):
        rounded = rest.astype(jnp.bfloat16).astype(jnp.float32)
        meta[part * tiles_dev : (part + 1) * tiles_dev, :] = rounded
        rest = rest - rounded
    ids = touch_ref[...]
    row = 3 * tiles_dev
    meta[row : row + tiles_dev, :touch_len] = (ids & 255).astype(jnp.float32)
    row += tiles_dev
    meta[row : row + tiles_dev, :touch_len] = (ids >> 8).astype(jnp.float32)
    row += tiles_dev
    meta[row : row + 1, :atoms] = rows_ref[...].astype(jnp.float32)
    out_ref[piece:] = meta[...].astype(jnp.bfloat16)
    copy.wait()


def weights_kernel(groups, at_ref, weight_ref, after_ref, across_ref, down_ref):
    per = across_ref.shape[1] // lanes
    for q in range(per):
        k = at_ref[0] * per + q
        start = pl.multiple_of(jnp.minimum(k, groups - 1) * lanes, lanes)
        value = jnp.where(k < groups, weight_ref[:, pl.ds(start, lanes)], 0.0)
        across_ref[:, q * lanes : (q + 1) * lanes] = value
        down_ref[q * lanes : (q + 1) * lanes, :] = jnp.broadcast_to(value, (lanes, lanes)).T


def tables_kernel(piece, tiles_dev, touch_len, keep, *refs):
    in_refs, outs = refs[:-6], refs[-6:]
    outer_ref, touch_ref, rows_ref, more_ref, raw, sems = outs
    low = len(in_refs) // 2
    copies = []
    for d in range(raw.shape[0]):
        y, k = d % low, d // low
        source = in_refs[2 * y + (k > 0)].at[max(k - 1, 0), piece:]
        copies.append(pltpu.make_async_copy(source, raw.at[d], sems.at[d]))
    for copy in copies:
        copy.start()
    for copy in copies:
        copy.wait()
    most = jnp.zeros((1, 1), jnp.float32)
    for d in range(raw.shape[0]):
        value = raw[d].astype(jnp.float32)
        span = slice(d * tiles_dev, (d + 1) * tiles_dev)
        parts = [value[p * tiles_dev : (p + 1) * tiles_dev] for p in range(5)]
        outer_ref[span, :] = parts[0] + parts[1] + parts[2]
        touch_ref[span, :] = (parts[3] + 256.0 * parts[4])[:, :touch_len].astype(jnp.int32)
        counts = value[5 * tiles_dev : 5 * tiles_dev + 1, : rows_ref.shape[1]]
        rows_ref[d : d + 1, :] = counts.astype(jnp.int32)
        most = jnp.maximum(most, jnp.sum(counts, axis=1, keepdims=True))
    more_ref[...] = (most > keep).astype(jnp.int32)


def load_basis(keys, basis_refs, basis, sems):
    copies = []
    for index, ref in enumerate(basis_refs):
        part, (y, e) = index % 2, keys[index // 2]
        target = basis.at[y, e, part : part + ref.shape[0]]
        copies.append(pltpu.make_async_copy(ref, target, sems.at[index]))
    for copy in copies:
        copy.start()
    return copies


def tile_blocks(touch_ref, index, blocks):
    return jnp.concatenate(
        [blocks[touch_ref[index, s]] for s in range(touch_ref.shape[1])], axis=0
    )


def tile_basis(beta, y, k, slot, tiles_dev, piece, basis):
    count = basis.shape[1] // tiles_dev
    parts = [basis[y, (slot * count + c) ^ beta, k, :piece] for c in range(count)]
    return jnp.concatenate(parts, axis=0)


def forward_kernel(plan, piece, scale, touch_ref, rows_ref, at_ref, weight_ref, *refs):
    n, keys, tiles_dev, first = plan
    k = 2 * len(keys)
    me, beta = at_ref[0], at_ref[1]
    if first:
        before_ref, block_ref, basis_refs = refs[0], refs[1], refs[2 : 2 + k]
        out_ref, blocks, basis, sems = refs[2 + k :]
    else:
        received, basis_refs = refs[:-4][: -k], refs[:-4][-k:]
        out_ref, blocks, basis, sems = refs[-4:]
    pad, width = blocks.shape[1:]
    atoms = blocks.shape[0] // n
    copies = load_basis(keys, basis_refs, basis, sems)
    if first:
        copies.append(pltpu.make_async_copy(block_ref, blocks, sems.at[k]))
        copies[-1].start()
        out_ref[...] = before_ref[...]
    else:
        for d in range(n):
            owner = me ^ d
            matrix = spread_matrix(lambda a: rows_ref[d, a], atoms, pad)
            packed = jnp.concatenate([ref[owner] for ref in received], axis=0)
            matrix = matrix[:, : packed.shape[0]]
            value = jnp.dot(matrix, packed, preferred_element_type=jnp.float32)
            value = value.astype(jnp.bfloat16).reshape(atoms, pad, width)
            blocks[pl.ds(owner * atoms, atoms)] = value
        out_ref[...] = jnp.zeros_like(out_ref)
    for copy in copies:
        copy.wait()

    low, m, size = basis.shape[:3]
    own = beta // (m // tiles_dev)

    def step(y, slots, index, carry):
        z, slot = index // len(slots), slots[0]
        if len(slots) > 1:
            slot = slots[0] + index % len(slots)
        slot = (slot + own) % tiles_dev
        values = tile_basis(beta, y, z, slot, tiles_dev, piece, basis)
        d = z * low + y
        part = tile_blocks(touch_ref, d * tiles_dev + slot, blocks)
        product = lax.dot_general(
            part, values, (((0,), (0,)), ((), ())), preferred_element_type=jnp.float32
        )
        orbital = product.astype(jnp.bfloat16).astype(jnp.float32)
        weight = jnp.concatenate([weight_ref[...]] * (orbital.shape[1] // lanes), axis=1)
        out_ref[pl.ds((d ^ me) * tiles_dev + slot, 1), :] = scale * jnp.sum(
            weight * orbital * orbital, axis=0, keepdims=True
        )
        return carry

    for y in range(1 if first else 0, low):
        slots = range(1, tiles_dev) if first else range(tiles_dev if y == 0 else 1)
        if slots:
            lax.fori_loop(
                0, size * len(slots), functools.partial(step, y, slots), 0, unroll=4
            )


def backward_kernel(
    n, k, tiles_dev, piece, touch_ref, rows_ref, at_ref, weight_ref, outer_ref, local_ref, *refs
):
    basis_refs, block_ref = refs[:k], refs[k]
    out_refs = refs[k + 1 : k + 1 + n]
    spill_ref, blocks, basis, total, sems = refs[k + 1 + n :]
    me, beta = at_ref[0], at_ref[1]
    tile_count, touch_len = touch_ref.shape
    pad, width = blocks.shape[1:]
    atoms = blocks.shape[0] // n
    held = pltpu.make_async_copy(block_ref, blocks, sems.at[k])
    held.start()
    keys = [(y, e) for y in range(basis.shape[0]) for e in range(basis.shape[1])]
    copies = load_basis(keys, basis_refs, basis, sems)
    total[...] = jnp.zeros_like(total)
    weight = weight_ref[...]
    held.wait()

    def step(y, index, carry):
        z, slot = index // tiles_dev, index % tiles_dev
        values = tile_basis(beta, y, z, slot, tiles_dev, piece, basis)
        d = z * basis.shape[0] + y
        row = d * tiles_dev + slot
        part = tile_blocks(touch_ref, row, blocks)
        potential = (
            outer_ref[pl.ds(row, 1), :] + local_ref[pl.ds((d ^ me) * tiles_dev + slot, 1), :]
        )
        scaled = (values.astype(jnp.float32) * potential).astype(jnp.bfloat16)
        couple = lax.dot_general(
            scaled, values, (((1,), (1,)), ((), ())), preferred_element_type=jnp.float32
        )
        high = couple.astype(jnp.bfloat16)
        low = (couple - high.astype(jnp.float32)).astype(jnp.bfloat16)
        product = jnp.dot(high, part, preferred_element_type=jnp.float32) + jnp.dot(
            low, part, preferred_element_type=jnp.float32
        )
        for s in range(touch_len):
            total[touch_ref[row, s]] += product[s * pad : (s + 1) * pad]
        return carry

    columns, each = basis.shape[0], len(copies) // basis.shape[0]
    for y in range(columns):
        for copy in copies[y * each : (y + 1) * each]:
            copy.wait()
        lax.fori_loop(0, tile_count // columns, functools.partial(step, y), 0, unroll=8)
    for d, out_ref in enumerate(out_refs):
        owner = me ^ d
        matrix = gather_matrix(lambda a: rows_ref[d, a], atoms, pad)
        value = total[pl.ds(owner * atoms, atoms)].reshape(atoms * pad, width)
        value = (weight * value).astype(jnp.bfloat16)
        packed = jnp.dot(matrix, value, preferred_element_type=jnp.float32).astype(jnp.bfloat16)
        out_ref[...] = packed[: out_ref.shape[0]]
        spill_ref[owner] = packed[out_ref.shape[0] :]


smem = pl.BlockSpec(memory_space=pltpu.SMEM)
vmem = pl.BlockSpec(memory_space=pltpu.VMEM)
anywhere = pl.BlockSpec(memory_space=pl.ANY)


def swap(value, axis, offset):
    size = lax.axis_size(axis)
    return lax.ppermute(value, axis, [(i, i ^ offset) for i in range(size)])


def exchange(parts):
    return [parts[0]] + [swap(parts[d], "grid", d) for d in range(1, len(parts))]


def all_sum(value):
    for axis in ("band", "grid"):
        offset = 1
        while offset < lax.axis_size(axis):
            value = value + swap(value, axis, offset)
            offset *= 2
    return value


def body(coefficients, block_rows, touch_atoms, basis_values, outer_field, occupations):
    n = lax.axis_size("grid")
    m = lax.axis_size("band")
    me = lax.axis_index("grid").astype(jnp.int32)
    beta = lax.axis_index("band").astype(jnp.int32)
    atoms, pad, band_dev = coefficients.shape
    tiles_dev, touch_len = touch_atoms.shape
    points = basis_values.shape[2]
    slots = basis_values.shape[1]
    tile_count = tiles_dev * n
    groups = band_dev // lanes
    per = (groups + n - 1) // n
    width = per * lanes
    params = pltpu.CompilerParams(vmem_limit_bytes=big_vmem)
    at = jnp.stack([me, beta])

    keep = atoms * pad * 13 // 16

    def across(value):
        return lax.all_to_all(value, "grid", split_axis=0, concat_axis=0, tiled=True)

    piece = tiles_dev * slots // m
    extra = -(-(5 * tiles_dev + 1) // 16) * 16
    low = 1 << ((n.bit_length() - 1) // 2)
    message = pl.pallas_call(
        functools.partial(prep_kernel, piece),
        out_shape=jax.ShapeDtypeStruct((piece + extra, points), jnp.bfloat16),
        in_specs=[smem, vmem, vmem, vmem, anywhere],
        out_specs=vmem,
        scratch_shapes=[pltpu.VMEM((extra, points), jnp.float32), pltpu.SemaphoreType.DMA],
        compiler_params=params,
        name="prep",
    )(
        at,
        touch_atoms,
        block_rows.reshape(1, atoms),
        outer_field,
        basis_values.reshape(tiles_dev * slots, points),
    )
    size = n // low
    pieces = {}

    def widen(h):
        for y in range(1, low):
            pieces[y, 0, h] = swap(pieces[0, 0, h], "grid", y)

    column = [message] + [swap(message, "grid", low * k) for k in range(1, size)]
    pieces[0, 0, 0] = message[None]
    widen(0)
    sent, spill = pl.pallas_call(
        functools.partial(pack_kernel, groups, per),
        out_shape=[
            jax.ShapeDtypeStruct((n, keep, width), jnp.bfloat16),
            jax.ShapeDtypeStruct((n, atoms * pad - keep, width), jnp.bfloat16),
        ],
        in_specs=[smem, vmem],
        out_specs=[vmem, vmem],
        compiler_params=params,
        name="pack",
    )(block_rows, coefficients)
    sent, spill, column, pieces = lax.optimization_barrier((sent, spill, column, pieces))
    got = across(sent)
    parts = [0, 1]
    pieces[0, 0, 1] = jnp.stack(column[1:])
    widen(1)
    cover = pl.CostEstimate(flops=0, bytes_accessed=1 << 27, transcendentals=0)
    weight, weight_down = pl.pallas_call(
        functools.partial(weights_kernel, groups),
        out_shape=[
            jax.ShapeDtypeStruct((1, width), jnp.float32),
            jax.ShapeDtypeStruct((width, lanes), jnp.float32),
        ],
        in_specs=[smem, vmem, anywhere],
        out_specs=[vmem] * 2,
        compiler_params=params,
        cost_estimate=cover,
        name="weights",
    )(at, occupations[None, :], pieces[0, 0, 1])
    count = m // tiles_dev
    last = [(y, x, 1) for y in range(1, low) for x in range(max(2, count), m, 2)]
    for h in parts:
        for y in range(low):
            for x in range(2, m, 2):
                if (y, x, h) not in last:
                    pieces[y, x, h] = swap(pieces[y, 0, h], "band", x)
    pieces, weight, weight_down = lax.optimization_barrier((pieces, weight, weight_down))
    for y, x, h in last:
        pieces[y, x, h] = swap(pieces[y, 0, h], "band", x)
    tables = [pieces[y, 0, h] for y in range(low) for h in parts]
    outer, touch, rows, more = pl.pallas_call(
        functools.partial(tables_kernel, piece, tiles_dev, touch_len, keep),
        out_shape=[
            jax.ShapeDtypeStruct((tile_count, points), jnp.float32),
            jax.ShapeDtypeStruct((tile_count, touch_len), jnp.int32),
            jax.ShapeDtypeStruct((n, atoms), jnp.int32),
            jax.ShapeDtypeStruct((1, 1), jnp.int32),
        ],
        in_specs=[anywhere] * len(tables),
        out_specs=[vmem] * 4,
        scratch_shapes=[
            pltpu.VMEM((n, extra, points), jnp.bfloat16),
            pltpu.SemaphoreType.DMA((n,)),
        ],
        compiler_params=params,
        name="tables",
    )(*tables)
    more = more[0, 0] > 0

    def rest(value):
        return lax.cond(more, across, lambda same: same, value)

    for y, x, h in list(pieces):
        if (y, x, h) not in last:
            pieces[y, x + 1, h] = swap(pieces[y, x, h], "band", 1)
    all_bands = band_dev * m
    held = jax.ShapeDtypeStruct((n * atoms, pad, width), jnp.bfloat16)
    value = jax.ShapeDtypeStruct((tile_count, points), jnp.float32)
    every = [(y, e) for y in range(low) for e in range(m)]
    far = [(y, e) for y, e in every if y > 0 and e >= count]
    near = [key for key in every if key not in far]

    def basis_of(keys):
        return [pieces[y, e, h] for y, e in keys for h in parts]

    def forward(keys, inputs):
        arrays = basis_of(keys)
        first = keys is far
        plan = (n, keys, tiles_dev, first)
        room = [
            pltpu.VMEM((low, m, size, piece + extra, points), jnp.bfloat16),
            pltpu.SemaphoreType.DMA((1 + len(arrays),)),
        ]
        places = [vmem, anywhere] if first else [vmem] * len(inputs)
        return pl.pallas_call(
            functools.partial(forward_kernel, plan, piece, 1.0 / all_bands),
            out_shape=value if first else [value, held],
            in_specs=[smem, smem, smem, vmem] + places + [anywhere] * len(arrays),
            out_specs=vmem if first else [vmem, vmem],
            scratch_shapes=[pltpu.VMEM(held.shape, held.dtype)] * first + room,
            compiler_params=params,
            cost_estimate=pl.CostEstimate(
                flops=2 * tile_count * len(keys) // len(every) * slots * width * points,
                bytes_accessed=1 << 27,
                transcendentals=0,
            ),
            name="forward",
        )(touch, rows, at, weight_down, *inputs, *arrays)

    partial_value, blocks = forward(near, [got])
    ends, partial_value, blocks = lax.optimization_barrier(
        ([pieces[k] for k in last], partial_value, blocks)
    )
    for (y, x, h), end in zip(last, ends):
        pieces[y, x, h] = end
        pieces[y, x + 1, h] = swap(end, "band", 1)
    partial_value = forward(far, [partial_value, blocks])

    def again(spill, *_):
        once, blocks = forward(near, [got, across(spill)])
        return forward(far, [once, blocks]), blocks

    partial_value, blocks = lax.cond(
        more, again, lambda spill, *same: same, spill, partial_value, blocks
    )
    basis = basis_of(every)
    count = len(basis)
    scratch = [
        pltpu.VMEM((n * atoms, pad, width), jnp.bfloat16),
        pltpu.VMEM((low, m, n // low, piece + extra, points), jnp.bfloat16),
    ]
    sems = pltpu.SemaphoreType.DMA((1 + count,))
    density = all_sum(partial_value)
    local = exchange_coef * jnp.cbrt(density)
    *back, spill = pl.pallas_call(
        functools.partial(backward_kernel, n, count, tiles_dev, piece),
        out_shape=[jax.ShapeDtypeStruct((keep, width), jnp.bfloat16)] * n
        + [jax.ShapeDtypeStruct((n, atoms * pad - keep, width), jnp.bfloat16)],
        in_specs=[smem, smem, smem, vmem, vmem, vmem] + [anywhere] * (1 + count),
        out_specs=[vmem] * (n + 1),
        scratch_shapes=scratch + [pltpu.VMEM((n * atoms, pad, width), jnp.float32), sems],
        compiler_params=params,
        name="backward",
    )(touch, rows, at, weight, outer, local, *basis, blocks)
    returned = exchange(back)
    spill = rest(spill)
    gradient = None
    half = n // 2
    early = [*range(half - 1), *range(half, n - n // 4), half - 1]
    for offsets in (early, range(n - n // 4, n)):
        before = [] if gradient is None else [gradient]
        gradient = pl.pallas_call(
            functools.partial(unpack_kernel, groups, per, tuple(offsets)),
            out_shape=jax.ShapeDtypeStruct((atoms, pad, band_dev), jnp.float32),
            in_specs=[smem, smem] + [vmem] * (1 + len(offsets)) + [anywhere] * len(before),
            out_specs=anywhere,
            scratch_shapes=[
                pltpu.VMEM((len(offsets), atoms, pad, width), jnp.float32),
                pltpu.SemaphoreType.DMA((len(offsets),)),
            ],
            input_output_aliases={3 + len(offsets): 0} if before else {},
            compiler_params=pltpu.CompilerParams(vmem_limit_bytes=big_vmem // 4),
            cost_estimate=pl.CostEstimate(flops=0, bytes_accessed=1 << 22, transcendentals=0),
            name="unpack",
        )(block_rows, at, spill, *[returned[d] for d in offsets], *before)
    own_density = lax.dynamic_slice_in_dim(density, me * tiles_dev, tiles_dev, 0)
    return (gradient, own_density)


def solution(mesh):
    placed = (
        P("grid", None, "band"),
        P("grid"),
        P("grid", None),
        P("grid", None, None),
        P("grid", None),
        P("band"),
    )
    return jax.shard_map(
        body,
        mesh=mesh,
        in_specs=placed,
        out_specs=(P("grid", None, "band"), P("grid", None)),
        check_vma=False,
    )
```

```python
import functools

import jax
import jax.numpy as jnp
from jax import lax
from jax.experimental import pallas as pl
from jax.experimental.pallas import tpu as pltpu
from jax.sharding import PartitionSpec as P

exchange_coef = -0.9847450218426965
lanes = 128
big_vmem = 60 * 1024 * 1024


def gather_matrix(rows, atoms, pad):
    count = atoms * pad
    lane = lax.broadcasted_iota(jnp.int32, (1, count), 1)
    place = jnp.full((1, count), -1, jnp.int32)
    start = 0
    for a in range(atoms):
        inner = lane - a * pad
        place = jnp.where((inner >= 0) & (inner < rows(a)), start + inner, place)
        start = start + rows(a)
    packed = lax.broadcasted_iota(jnp.int32, (count, count), 0)
    return jnp.where(packed == place, 1.0, 0.0).astype(jnp.bfloat16)


def spread_matrix(rows, atoms, pad):
    inner = lax.broadcasted_iota(jnp.int32, (pad, atoms * pad), 0)
    packed = lax.broadcasted_iota(jnp.int32, (pad, atoms * pad), 1)
    parts = []
    start = 0
    for a in range(atoms):
        parts.append(jnp.where((packed == start + inner) & (inner < rows(a)), 1.0, 0.0))
        start = start + rows(a)
    return jnp.concatenate(parts, axis=0).astype(jnp.bfloat16)


def pack_kernel(groups, per, rows_ref, coef_ref, main_ref, spill_ref):
    atoms, pad, band_dev = coef_ref.shape
    n, keep, width = main_ref.shape
    matrix = gather_matrix(lambda a: rows_ref[a], atoms, pad)
    for j in range(n):
        used = max(0, min(width, band_dev - j * width))
        if used:
            value = coef_ref[:, :, j * width : j * width + used].reshape(atoms * pad, used)
            packed = jnp.dot(matrix, value, preferred_element_type=jnp.float32)
            packed = packed.astype(jnp.bfloat16)
            main_ref[j, :, :used] = packed[:keep]
            spill_ref[j, :, :used] = packed[keep:]
        if used < width:
            main_ref[j, :, used:] = jnp.zeros((keep, width - used), jnp.bfloat16)
            spill_ref[j, :, used:] = jnp.zeros((atoms * pad - keep, width - used), jnp.bfloat16)


def unpack_kernel(groups, per, offsets, rows_ref, at_ref, spill_ref, *refs):
    in_refs, (out_ref, values, sems) = refs[: len(offsets)], refs[-3:]
    me = at_ref[0]
    atoms, pad, _ = out_ref.shape
    matrix = spread_matrix(lambda a: rows_ref[a], atoms, pad)
    whole, rest = groups // per, groups % per * lanes
    copies = []
    for index, in_ref in enumerate(in_refs):
        peer = me ^ offsets[index]
        packed = jnp.concatenate([in_ref[...], spill_ref[peer]], axis=0)
        value = jnp.dot(matrix, packed, preferred_element_type=jnp.float32)
        values[index] = value.reshape(values.shape[1:])
        start = pl.multiple_of(peer * (per * lanes), lanes)
        for used, there in ((per * lanes, peer < whole), (rest, peer == whole)):
            if used:
                target = out_ref.at[:, :, pl.ds(jnp.where(there, start, 0), used)]
                copy = pltpu.make_async_copy(
                    values.at[index, :, :, :used], target, sems.at[index]
                )
                copies.append((there, copy))
                pl.when(there)(copy.start)
    for there, copy in copies:
        pl.when(there)(copy.wait)


def prep_kernel(piece, at_ref, touch_ref, rows_ref, outer_ref, basis_ref, out_ref, meta, sem):
    beta = at_ref[1]
    tiles_dev, touch_len = touch_ref.shape
    atoms = rows_ref.shape[1]
    start = pl.multiple_of(beta * piece, piece)
    copy = pltpu.make_async_copy(basis_ref.at[pl.ds(start, piece)], out_ref.at[:piece], sem)
    copy.start()
    meta[...] = jnp.zeros_like(meta)
    rest = outer_ref[...]
    for part in range(3):
        rounded = rest.astype(jnp.bfloat16).astype(jnp.float32)
        meta[part * tiles_dev : (part + 1) * tiles_dev, :] = rounded
        rest = rest - rounded
    ids = touch_ref[...]
    row = 3 * tiles_dev
    meta[row : row + tiles_dev, :touch_len] = (ids & 255).astype(jnp.float32)
    row += tiles_dev
    meta[row : row + tiles_dev, :touch_len] = (ids >> 8).astype(jnp.float32)
    row += tiles_dev
    meta[row : row + 1, :atoms] = rows_ref[...].astype(jnp.float32)
    out_ref[piece:] = meta[...].astype(jnp.bfloat16)
    copy.wait()


def weights_kernel(groups, at_ref, weight_ref, after_ref, across_ref, down_ref):
    per = across_ref.shape[1] // lanes
    for q in range(per):
        k = at_ref[0] * per + q
        start = pl.multiple_of(jnp.minimum(k, groups - 1) * lanes, lanes)
        value = jnp.where(k < groups, weight_ref[:, pl.ds(start, lanes)], 0.0)
        across_ref[:, q * lanes : (q + 1) * lanes] = value
        down_ref[q * lanes : (q + 1) * lanes, :] = jnp.broadcast_to(value, (lanes, lanes)).T


def tables_kernel(piece, tiles_dev, touch_len, keep, *refs):
    in_refs, outs = refs[:-6], refs[-6:]
    outer_ref, touch_ref, rows_ref, more_ref, raw, sems = outs
    low = len(in_refs) // 2
    copies = []
    for d in range(raw.shape[0]):
        y, k = d % low, d // low
        source = in_refs[2 * y + (k > 0)].at[max(k - 1, 0), piece:]
        copies.append(pltpu.make_async_copy(source, raw.at[d], sems.at[d]))
    for copy in copies:
        copy.start()
    for copy in copies:
        copy.wait()
    most = jnp.zeros((1, 1), jnp.float32)
    for d in range(raw.shape[0]):
        value = raw[d].astype(jnp.float32)
        span = slice(d * tiles_dev, (d + 1) * tiles_dev)
        parts = [value[p * tiles_dev : (p + 1) * tiles_dev] for p in range(5)]
        outer_ref[span, :] = parts[0] + parts[1] + parts[2]
        touch_ref[span, :] = (parts[3] + 256.0 * parts[4])[:, :touch_len].astype(jnp.int32)
        counts = value[5 * tiles_dev : 5 * tiles_dev + 1, : rows_ref.shape[1]]
        rows_ref[d : d + 1, :] = counts.astype(jnp.int32)
        most = jnp.maximum(most, jnp.sum(counts, axis=1, keepdims=True))
    more_ref[...] = (most > keep).astype(jnp.int32)


def load_basis(keys, basis_refs, basis, sems):
    copies = []
    for index, ref in enumerate(basis_refs):
        part, (y, e) = index % 2, keys[index // 2]
        target = basis.at[y, e, part : part + ref.shape[0]]
        copies.append(pltpu.make_async_copy(ref, target, sems.at[index]))
    for copy in copies:
        copy.start()
    return copies


def tile_blocks(touch_ref, index, blocks):
    return jnp.concatenate(
        [blocks[touch_ref[index, s]] for s in range(touch_ref.shape[1])], axis=0
    )


def tile_basis(beta, y, k, slot, tiles_dev, piece, basis):
    count = basis.shape[1] // tiles_dev
    parts = [basis[y, (slot * count + c) ^ beta, k, :piece] for c in range(count)]
    return jnp.concatenate(parts, axis=0)


def forward_kernel(plan, piece, scale, touch_ref, rows_ref, at_ref, weight_ref, *refs):
    n, keys, tiles_dev, first = plan
    k = 2 * len(keys)
    me, beta = at_ref[0], at_ref[1]
    if first:
        before_ref, block_ref, basis_refs = refs[0], refs[1], refs[2 : 2 + k]
        out_ref, blocks, basis, sems = refs[2 + k :]
    else:
        received, basis_refs = refs[:-4][: -k], refs[:-4][-k:]
        out_ref, blocks, basis, sems = refs[-4:]
    pad, width = blocks.shape[1:]
    atoms = blocks.shape[0] // n
    copies = load_basis(keys, basis_refs, basis, sems)
    if first:
        copies.append(pltpu.make_async_copy(block_ref, blocks, sems.at[k]))
        copies[-1].start()
        out_ref[...] = before_ref[...]
    else:
        for d in range(n):
            owner = me ^ d
            matrix = spread_matrix(lambda a: rows_ref[d, a], atoms, pad)
            packed = jnp.concatenate([ref[owner] for ref in received], axis=0)
            matrix = matrix[:, : packed.shape[0]]
            value = jnp.dot(matrix, packed, preferred_element_type=jnp.float32)
            value = value.astype(jnp.bfloat16).reshape(atoms, pad, width)
            blocks[pl.ds(owner * atoms, atoms)] = value
        out_ref[...] = jnp.zeros_like(out_ref)
    for copy in copies:
        copy.wait()

    low, m, size = basis.shape[:3]
    own = beta // (m // tiles_dev)

    def step(y, slots, index, carry):
        z, slot = index // len(slots), slots[0]
        if len(slots) > 1:
            slot = slots[0] + index % len(slots)
        slot = (slot + own) % tiles_dev
        values = tile_basis(beta, y, z, slot, tiles_dev, piece, basis)
        d = z * low + y
        part = tile_blocks(touch_ref, d * tiles_dev + slot, blocks)
        product = lax.dot_general(
            part, values, (((0,), (0,)), ((), ())), preferred_element_type=jnp.float32
        )
        orbital = product.astype(jnp.bfloat16).astype(jnp.float32)
        weight = jnp.concatenate([weight_ref[...]] * (orbital.shape[1] // lanes), axis=1)
        out_ref[pl.ds((d ^ me) * tiles_dev + slot, 1), :] = scale * jnp.sum(
            weight * orbital * orbital, axis=0, keepdims=True
        )
        return carry

    for y in range(1 if first else 0, low):
        slots = range(1, tiles_dev) if first else range(tiles_dev if y == 0 else 1)
        if slots:
            lax.fori_loop(
                0, size * len(slots), functools.partial(step, y, slots), 0, unroll=4
            )


def backward_kernel(
    n, k, tiles_dev, piece, touch_ref, rows_ref, at_ref, weight_ref, outer_ref, local_ref, *refs
):
    basis_refs, block_ref = refs[:k], refs[k]
    out_refs = refs[k + 1 : k + 1 + n]
    spill_ref, blocks, basis, total, sems = refs[k + 1 + n :]
    me, beta = at_ref[0], at_ref[1]
    tile_count, touch_len = touch_ref.shape
    pad, width = blocks.shape[1:]
    atoms = blocks.shape[0] // n
    held = pltpu.make_async_copy(block_ref, blocks, sems.at[k])
    held.start()
    keys = [(y, e) for y in range(basis.shape[0]) for e in range(basis.shape[1])]
    copies = load_basis(keys, basis_refs, basis, sems)
    total[...] = jnp.zeros_like(total)
    weight = weight_ref[...]
    held.wait()

    def step(y, index, carry):
        z, slot = index // tiles_dev, index % tiles_dev
        values = tile_basis(beta, y, z, slot, tiles_dev, piece, basis)
        d = z * basis.shape[0] + y
        row = d * tiles_dev + slot
        part = tile_blocks(touch_ref, row, blocks)
        potential = (
            outer_ref[pl.ds(row, 1), :] + local_ref[pl.ds((d ^ me) * tiles_dev + slot, 1), :]
        )
        scaled = (values.astype(jnp.float32) * potential).astype(jnp.bfloat16)
        couple = lax.dot_general(
            scaled, values, (((1,), (1,)), ((), ())), preferred_element_type=jnp.float32
        )
        high = couple.astype(jnp.bfloat16)
        low = (couple - high.astype(jnp.float32)).astype(jnp.bfloat16)
        product = jnp.dot(high, part, preferred_element_type=jnp.float32) + jnp.dot(
            low, part, preferred_element_type=jnp.float32
        )
        for s in range(touch_len):
            total[touch_ref[row, s]] += product[s * pad : (s + 1) * pad]
        return carry

    columns, each = basis.shape[0], len(copies) // basis.shape[0]
    for y in range(columns):
        for copy in copies[y * each : (y + 1) * each]:
            copy.wait()
        lax.fori_loop(0, tile_count // columns, functools.partial(step, y), 0, unroll=8)
    for d, out_ref in enumerate(out_refs):
        owner = me ^ d
        matrix = gather_matrix(lambda a: rows_ref[d, a], atoms, pad)
        value = total[pl.ds(owner * atoms, atoms)].reshape(atoms * pad, width)
        value = (weight * value).astype(jnp.bfloat16)
        packed = jnp.dot(matrix, value, preferred_element_type=jnp.float32).astype(jnp.bfloat16)
        out_ref[...] = packed[: out_ref.shape[0]]
        spill_ref[owner] = packed[out_ref.shape[0] :]


smem = pl.BlockSpec(memory_space=pltpu.SMEM)
vmem = pl.BlockSpec(memory_space=pltpu.VMEM)
anywhere = pl.BlockSpec(memory_space=pl.ANY)


def swap(value, axis, offset):
    size = lax.axis_size(axis)
    return lax.ppermute(value, axis, [(i, i ^ offset) for i in range(size)])


def exchange(parts):
    return [parts[0]] + [swap(parts[d], "grid", d) for d in range(1, len(parts))]


def all_sum(value):
    for axis in ("band", "grid"):
        offset = 1
        while offset < lax.axis_size(axis):
            value = value + swap(value, axis, offset)
            offset *= 2
    return value


def body(coefficients, block_rows, touch_atoms, basis_values, outer_field, occupations):
    n = lax.axis_size("grid")
    m = lax.axis_size("band")
    me = lax.axis_index("grid").astype(jnp.int32)
    beta = lax.axis_index("band").astype(jnp.int32)
    atoms, pad, band_dev = coefficients.shape
    tiles_dev, touch_len = touch_atoms.shape
    points = basis_values.shape[2]
    slots = basis_values.shape[1]
    tile_count = tiles_dev * n
    groups = band_dev // lanes
    per = (groups + n - 1) // n
    width = per * lanes
    params = pltpu.CompilerParams(vmem_limit_bytes=big_vmem)
    at = jnp.stack([me, beta])

    keep = atoms * pad * 13 // 16

    def across(value):
        return lax.all_to_all(value, "grid", split_axis=0, concat_axis=0, tiled=True)

    piece = tiles_dev * slots // m
    extra = -(-(5 * tiles_dev + 1) // 16) * 16
    low = 1 << ((n.bit_length() - 1) // 2)
    message = pl.pallas_call(
        functools.partial(prep_kernel, piece),
        out_shape=jax.ShapeDtypeStruct((piece + extra, points), jnp.bfloat16),
        in_specs=[smem, vmem, vmem, vmem, anywhere],
        out_specs=vmem,
        scratch_shapes=[pltpu.VMEM((extra, points), jnp.float32), pltpu.SemaphoreType.DMA],
        compiler_params=params,
        name="prep",
    )(
        at,
        touch_atoms,
        block_rows.reshape(1, atoms),
        outer_field,
        basis_values.reshape(tiles_dev * slots, points),
    )
    size = n // low
    pieces = {}

    def widen(h):
        for y in range(1, low):
            pieces[y, 0, h] = swap(pieces[0, 0, h], "grid", y)

    column = [message] + [swap(message, "grid", low * k) for k in range(1, size)]
    pieces[0, 0, 0] = message[None]
    widen(0)
    sent, spill = pl.pallas_call(
        functools.partial(pack_kernel, groups, per),
        out_shape=[
            jax.ShapeDtypeStruct((n, keep, width), jnp.bfloat16),
            jax.ShapeDtypeStruct((n, atoms * pad - keep, width), jnp.bfloat16),
        ],
        in_specs=[smem, vmem],
        out_specs=[vmem, vmem],
        compiler_params=params,
        name="pack",
    )(block_rows, coefficients)
    sent, spill, column, pieces = lax.optimization_barrier((sent, spill, column, pieces))
    got = across(sent)
    parts = [0, 1]
    pieces[0, 0, 1] = jnp.stack(column[1:])
    widen(1)
    cover = pl.CostEstimate(flops=0, bytes_accessed=1 << 27, transcendentals=0)
    weight, weight_down = pl.pallas_call(
        functools.partial(weights_kernel, groups),
        out_shape=[
            jax.ShapeDtypeStruct((1, width), jnp.float32),
            jax.ShapeDtypeStruct((width, lanes), jnp.float32),
        ],
        in_specs=[smem, vmem, anywhere],
        out_specs=[vmem] * 2,
        compiler_params=params,
        cost_estimate=cover,
        name="weights",
    )(at, occupations[None, :], pieces[0, 0, 1])
    count = m // tiles_dev
    last = [(y, x, 1) for y in range(1, low) for x in range(max(2, count), m, 2)]
    for h in parts:
        for y in range(low):
            for x in range(2, m, 2):
                if (y, x, h) not in last:
                    pieces[y, x, h] = swap(pieces[y, 0, h], "band", x)
    pieces, weight, weight_down = lax.optimization_barrier((pieces, weight, weight_down))
    for y, x, h in last:
        pieces[y, x, h] = swap(pieces[y, 0, h], "band", x)
    tables = [pieces[y, 0, h] for y in range(low) for h in parts]
    outer, touch, rows, more = pl.pallas_call(
        functools.partial(tables_kernel, piece, tiles_dev, touch_len, keep),
        out_shape=[
            jax.ShapeDtypeStruct((tile_count, points), jnp.float32),
            jax.ShapeDtypeStruct((tile_count, touch_len), jnp.int32),
            jax.ShapeDtypeStruct((n, atoms), jnp.int32),
            jax.ShapeDtypeStruct((1, 1), jnp.int32),
        ],
        in_specs=[anywhere] * len(tables),
        out_specs=[vmem] * 4,
        scratch_shapes=[
            pltpu.VMEM((n, extra, points), jnp.bfloat16),
            pltpu.SemaphoreType.DMA((n,)),
        ],
        compiler_params=params,
        name="tables",
    )(*tables)
    more = more[0, 0] > 0

    def rest(value):
        return lax.cond(more, across, lambda same: same, value)

    for y, x, h in list(pieces):
        if (y, x, h) not in last:
            pieces[y, x + 1, h] = swap(pieces[y, x, h], "band", 1)
    all_bands = band_dev * m
    held = jax.ShapeDtypeStruct((n * atoms, pad, width), jnp.bfloat16)
    value = jax.ShapeDtypeStruct((tile_count, points), jnp.float32)
    every = [(y, e) for y in range(low) for e in range(m)]
    far = [(y, e) for y, e in every if y > 0 and e >= count]
    near = [key for key in every if key not in far]

    def basis_of(keys):
        return [pieces[y, e, h] for y, e in keys for h in parts]

    def forward(keys, inputs):
        arrays = basis_of(keys)
        first = keys is far
        plan = (n, keys, tiles_dev, first)
        room = [
            pltpu.VMEM((low, m, size, piece + extra, points), jnp.bfloat16),
            pltpu.SemaphoreType.DMA((1 + len(arrays),)),
        ]
        places = [vmem, anywhere] if first else [vmem] * len(inputs)
        return pl.pallas_call(
            functools.partial(forward_kernel, plan, piece, 1.0 / all_bands),
            out_shape=value if first else [value, held],
            in_specs=[smem, smem, smem, vmem] + places + [anywhere] * len(arrays),
            out_specs=vmem if first else [vmem, vmem],
            scratch_shapes=[pltpu.VMEM(held.shape, held.dtype)] * first + room,
            compiler_params=pltpu.CompilerParams(vmem_limit_bytes=big_vmem // 2),
            cost_estimate=pl.CostEstimate(
                flops=2 * tile_count * len(keys) // len(every) * slots * width * points,
                bytes_accessed=1 << 27,
                transcendentals=0,
            ),
            name="forward",
        )(touch, rows, at, weight_down, *inputs, *arrays)

    partial_value, blocks = forward(near, [got])
    ends, partial_value, blocks = lax.optimization_barrier(
        ([pieces[k] for k in last], partial_value, blocks)
    )
    for (y, x, h), end in zip(last, ends):
        pieces[y, x, h] = end
        pieces[y, x + 1, h] = swap(end, "band", 1)
    partial_value = forward(far, [partial_value, blocks])

    def again(spill, *_):
        once, blocks = forward(near, [got, across(spill)])
        return forward(far, [once, blocks]), blocks

    partial_value, blocks = lax.cond(
        more, again, lambda spill, *same: same, spill, partial_value, blocks
    )
    basis = basis_of(every)
    count = len(basis)
    scratch = [
        pltpu.VMEM((n * atoms, pad, width), jnp.bfloat16),
        pltpu.VMEM((low, m, n // low, piece + extra, points), jnp.bfloat16),
    ]
    sems = pltpu.SemaphoreType.DMA((1 + count,))
    density = all_sum(partial_value)
    local = exchange_coef * jnp.cbrt(density)
    *back, spill = pl.pallas_call(
        functools.partial(backward_kernel, n, count, tiles_dev, piece),
        out_shape=[jax.ShapeDtypeStruct((keep, width), jnp.bfloat16)] * n
        + [jax.ShapeDtypeStruct((n, atoms * pad - keep, width), jnp.bfloat16)],
        in_specs=[smem, smem, smem, vmem, vmem, vmem] + [anywhere] * (1 + count),
        out_specs=[vmem] * (n + 1),
        scratch_shapes=scratch + [pltpu.VMEM((n * atoms, pad, width), jnp.float32), sems],
        compiler_params=params,
        name="backward",
    )(touch, rows, at, weight, outer, local, *basis, blocks)
    returned = exchange(back)
    spill = rest(spill)
    gradient = None
    half = n // 2
    early = [*range(half - 1), *range(half, n - n // 4), half - 1]
    for offsets in (early, range(n - n // 4, n)):
        before = [] if gradient is None else [gradient]
        gradient = pl.pallas_call(
            functools.partial(unpack_kernel, groups, per, tuple(offsets)),
            out_shape=jax.ShapeDtypeStruct((atoms, pad, band_dev), jnp.float32),
            in_specs=[smem, smem] + [vmem] * (1 + len(offsets)) + [anywhere] * len(before),
            out_specs=anywhere,
            scratch_shapes=[
                pltpu.VMEM((len(offsets), atoms, pad, width), jnp.float32),
                pltpu.SemaphoreType.DMA((len(offsets),)),
            ],
            input_output_aliases={3 + len(offsets): 0} if before else {},
            compiler_params=pltpu.CompilerParams(vmem_limit_bytes=big_vmem // 4),
            cost_estimate=pl.CostEstimate(flops=0, bytes_accessed=1 << 22, transcendentals=0),
            name="unpack",
        )(block_rows, at, spill, *[returned[d] for d in offsets], *before)
    own_density = lax.dynamic_slice_in_dim(density, me * tiles_dev, tiles_dev, 0)
    return (gradient, own_density)


def solution(mesh):
    placed = (
        P("grid", None, "band"),
        P("grid"),
        P("grid", None),
        P("grid", None, None),
        P("grid", None),
        P("band"),
    )
    return jax.shard_map(
        body,
        mesh=mesh,
        in_specs=placed,
        out_specs=(P("grid", None, "band"), P("grid", None)),
        check_vma=False,
    )
```
